32 devices in a mesh: member: 2 (over x), wave: 8 (over z, y), lev: 2 (over core).
Axes of the slice: x: 2, y: 2, z: 4, core: 2. Of those that a mesh axis runs over, the one named last changes fastest.
Arguments:
- grid: bfloat16 [128, 320, 2, 1280], P(('member', 'lev'), 'wave'), parts along dimension 0, may hold values from -6 to 6
- lat_order: int32 [320], replicated, may hold values from 0 to 319, each once
- wave_order: int32 [640], replicated, may hold values from 0 to 639, as said below
- trim: int32 [640], replicated, may hold values from 0 to 4, as said below
- legendre: bfloat16 [640, 640, 320], P('wave'), may hold values from -0.3125 to 0.3125
- modes_in: bfloat16 [64, 64], replicated, may hold values from -0.75 to 0.75
- modes_out: bfloat16 [64, 64], replicated, may hold values from -0.75 to 0.75
- implicit: float32 [64], replicated, may hold values from 0.3 to 30
Outputs:
- fourier_out: bfloat16 [128, 320, 2, 1280], P(('member', 'lev'), 'wave'), parts along dimension 0
The draws below stay inside these ranges and needn't reach their ends.
There are 2 independent parts, one for each index of `member`. The reference program is written for one: setup_inputs(seed, part) draws one part's arguments, and reference() takes and returns one part's arrays. A program takes and returns all parts, laid end to end along the dimension named above; an argument that names none is the same for every part. Nothing has to cross between parts.
Inputs may be any that keep to these rules, and one draw needn't show every extreme that they name: `wave_order`: a permutation of 0 to 639 in which entries 2i and 2i+1 are k and 639-k for some k. `trim`: for wavenumber m, how many blocks of 64 latitudes nearest each pole take no part in its products.
All inputs are finite; a program needn't handle non-finite values.
Results may differ from the reference program's by a relative error of at most 0.015.
Values may be sent and summed in bfloat16 or wider, within the bound.
No kernel may reach another device: no remote copies, remote signals or barrier semaphores. Data moves between devices by JAX's collectives and lax.ppermute only.
A program may use at most 192 MiB of HBM per device.

```python
import math
import jax
import jax.numpy as jnp
from jax import lax

F = 64
NLON = 1280
M = 640
HALF = 320
LBLK = 64


def draw_wave_order(key, part):
    pair_first = jax.random.permutation(key, M // 2).astype(jnp.int32)
    return jnp.stack([pair_first, M - 1 - pair_first], 1).reshape(M).astype(jnp.int32)


def draw_trim(key, part):
    blocks = HALF // LBLK
    base_blocks = jnp.arange(M, dtype=jnp.int32) * blocks // M
    jitter = jax.random.randint(jax.random.fold_in(key, 7), (M,), 0, 2, dtype=jnp.int32)
    drawn_trim = jnp.clip(base_blocks - jitter, 0, blocks - 1)
    return drawn_trim.at[M - 1].set(blocks - 1).astype(jnp.int32)


def block_scale(rng, extent, cuts, low, largest):
    gain, own = 1.0, jax.random.fold_in(rng, 6)
    for position, parts in cuts:
        draws = jnp.exp(jax.random.uniform(jax.random.fold_in(own, position), (parts,), jnp.float32, low / len(cuts), largest / len(cuts)))
        gain = gain * jnp.repeat(draws, extent[position] // parts).reshape([-1 if axis == position else 1 for axis in range(len(extent))])
    return gain


def gaussian(stream_key, shape, scale, bound, shards=(), kind=jnp.bfloat16):
    drawn = jax.random.normal(stream_key, shape, jnp.float32) * scale
    if len(shards) > 0:
        drawn = block_scale(stream_key, shape, shards, -0.22, 0.18) * drawn
    return jnp.clip(drawn, min=-bound, max=bound).astype(kind)


def setup_inputs(seed: int = 0, part: int = 0) -> dict:
    keys = jax.random.split(jax.random.key(seed), 9)
    part_splits = jax.random.split(jax.random.fold_in(keys[8], part), 9)
    return {
        "grid": gaussian(part_splits[0], (F, HALF, 2, NLON), 1.0, 6.0, ((0, 2), (1, 8))),
        "lat_order": jax.random.permutation(keys[1], HALF).astype(jnp.int32),
        "wave_order": draw_wave_order(jax.random.fold_in(keys[8], 71), part),
        "trim": draw_trim(jax.random.fold_in(keys[8], 71), part),
        "legendre": gaussian(keys[4], (M, M, HALF), HALF ** -0.5, 0.3125, ((0, 8),)),
        "modes_in": gaussian(keys[5], (F, F), F ** -0.5, 0.75),
        "modes_out": gaussian(keys[6], (F, F), F ** -0.5, 0.75),
        "implicit": jnp.clip(jnp.exp(jax.random.uniform(keys[7], (F,), jnp.float32, math.log(0.3), math.log(30.0))), 0.3, 30.0),
    }


def reference(grid, lat_order, wave_order, trim, legendre, modes_in, modes_out, implicit):
    spectra = jnp.fft.rfft(grid.astype(jnp.float32), axis=3)[..., :M] / math.sqrt(NLON)
    picked = spectra[..., wave_order]
    fourier = jnp.stack([jnp.real(picked), jnp.imag(picked)], -1).reshape(F, HALF, 2, 2 * M).astype(jnp.bfloat16)
    fourier = lax.optimization_barrier(fourier).astype(jnp.float32)
    symmetric = jnp.stack([fourier[:, :, 0] + fourier[:, :, 1], fourier[:, :, 0] - fourier[:, :, 1]], 2).astype(jnp.bfloat16)
    inverse_order = jnp.zeros((HALF,), jnp.int32).at[lat_order].set(jnp.arange(HALF, dtype=jnp.int32))
    physical = symmetric[:, inverse_order]
    latitude = jnp.arange(HALF, dtype=jnp.int32)
    row_index = jnp.arange(M, dtype=jnp.int32)

    def one_slot(slot_index):
        wavenum = wave_order[slot_index]
        keep_mask = (wavenum + row_index < M)[:, None] & (latitude >= LBLK * trim[wavenum])[None, :]
        lat_basis = jnp.where(keep_mask, legendre[slot_index].astype(jnp.float32), jnp.float32(0.0)).reshape(M // 2, 2, HALF)
        slot_data = lax.dynamic_slice_in_dim(physical, 2 * slot_index, 2, 3).astype(jnp.float32)
        coeffs = jnp.einsum('aej,fjec->aecf', lat_basis, slot_data).astype(jnp.bfloat16)
        degree = (wavenum + row_index).astype(jnp.float32).reshape(M // 2, 2)
        factor = degree * (degree + 1.0) / float(M * (M - 1))
        modal_part = jnp.einsum('kl,aecl->aeck', modes_in.astype(jnp.float32), coeffs.astype(jnp.float32))
        scaled = (modal_part / (1.0 + factor[:, :, None, None] * implicit)).astype(jnp.bfloat16)
        solved = jnp.einsum('lk,aeck->aecl', modes_out.astype(jnp.float32), scaled.astype(jnp.float32)).astype(jnp.bfloat16)
        parity_sums = jnp.einsum('aej,aecl->ejcl', lat_basis, solved.astype(jnp.float32))
        hemispheres = jnp.stack([parity_sums[0] + parity_sums[1], parity_sums[0] - parity_sums[1]], 1)
        return hemispheres.astype(jnp.bfloat16)
    results = lax.map(one_slot, jnp.arange(M, dtype=jnp.int32))
    ordered = results[:, lat_order]
    return ordered.transpose(4, 1, 2, 0, 3).reshape(F, HALF, 2, 2 * M)
```

```python
import functools
import math

import jax
import jax.numpy as jnp
from jax import lax
from jax.experimental import pallas as pl
from jax.experimental.pallas import tpu as pltpu
from jax.sharding import PartitionSpec as P

LBLK = 64
LANES = 128
TILE = 8
AXES = ("wave", "lev")
NT = (((1,), (1,)), ((), ()))
NN = (((1,), (0,)), ((), ()))


def dot(a, b, dims=NN):
    return lax.dot_general(a, b, dims, preferred_element_type=jnp.float32)


def cosine_rows(freq_ref, first, count, width, lon_count):
    freq = freq_ref[pl.ds(first, count), :]
    row = lax.broadcasted_iota(jnp.int32, (count, 1), 0) + first
    phase = ((row // width) % 2).astype(jnp.float32) * (lon_count // 4)
    longitude = lax.broadcasted_iota(jnp.int32, (count, lon_count), 1).astype(jnp.float32)
    turns = freq * longitude + phase
    whole = jnp.floor(turns * (1.0 / lon_count) + 0.5)
    rest = jnp.abs(turns - whole * lon_count) * (1.0 / lon_count)
    angle = (0.25 - rest) * (2.0 * math.pi)
    square = angle * angle
    value = jnp.full_like(square, -1.0 / 39916800.0)
    for term in (1.0 / 362880.0, -1.0 / 5040.0, 1.0 / 120.0, -1.0 / 6.0, 1.0):
        value = value * square + term
    return (value * angle * (1.0 / math.sqrt(lon_count))).astype(jnp.bfloat16)


def dft_kernel(lats_ref, grid_ref, *refs, widths, low, pairs):
    count = len(widths)
    freqs, outs, tables = refs[:count], refs[count : 2 * count], refs[2 * count :]
    lon_count = grid_ref.shape[3]

    @pl.when(pl.program_id(0) == 0)
    def _():
        for freq, table, width in zip(freqs, tables, widths):
            step = 2 * width

            @pl.loop(0, table.shape[0] // step)
            def _(i):
                first = pl.multiple_of(i * step, step)
                table[pl.ds(first, step), :] = cosine_rows(freq, first, step, width, lon_count)

    fields = grid_ref.shape[0]
    rows = []
    for slot in range(pairs * low):
        rows.append(grid_ref[:, slot].reshape(2 * fields, lon_count))
    values = jnp.concatenate(rows, 0)
    for out, table, width in zip(outs, tables, widths):
        spectra = dot(table[...], values, NT)
        for pair in range(pairs):
            part = spectra[:, pair * LANES : (pair + 1) * LANES]
            out[:, :, pair] = part.reshape(-1, 2, width, LANES).astype(jnp.bfloat16)


def dft(grid, freqs, widths, owners, low):
    fields, lats, _, lon_count = grid.shape
    count = lats // low
    pairs = 2 if count % 2 == 0 else 1
    lats_order = jnp.arange(lats, dtype=jnp.int32)
    specs = [pl.BlockSpec((fields, pairs * low, 2, lon_count), lambda i, _: (0, i, 0, 0))]
    specs += [pl.BlockSpec(f.shape, lambda i, _: (0, 0)) for f in freqs]
    return pl.pallas_call(
        functools.partial(dft_kernel, widths=widths, low=low, pairs=pairs),
        grid_spec=pltpu.PrefetchScalarGridSpec(
            num_scalar_prefetch=1,
            grid=(count // pairs,),
            in_specs=specs,
            out_specs=[
                pl.BlockSpec((owners, 2, pairs, w, LANES), lambda i, _: (0, 0, i, 0, 0))
                for w in widths
            ],
            scratch_shapes=[pltpu.VMEM((f.shape[0], lon_count), jnp.bfloat16) for f in freqs],
        ),
        out_shape=[
            jax.ShapeDtypeStruct((owners, 2, count, w, LANES), jnp.bfloat16) for w in widths
        ],
        name="dft",
    )(lats_order, grid, *freqs)


def middle_kernel(meta, data, legendre, select, into, back, implicit, out, held, made, *, levels):
    step = pl.program_id(0)
    owners, _, count, width, _ = data.shape
    groups = owners // levels
    half = LANES // 2
    lat_count, row_count = legendre.shape[1], legendre.shape[2]

    @pl.when(step == 0)
    def _():
        for owner in range(owners):
            group, level = owner // levels, owner % levels
            for part in range(2):
                first = ((level * 2 + part) * groups + group) * count
                block = data[owner, part].astype(jnp.float32)
                held[pl.ds(first * width, count * width), :] = block.reshape(-1, LANES)

    wavenum, trim = meta[0, step], meta[1, step]
    slots = groups * count
    north, south = [], []
    for combo in range(2 * levels):
        block = held[pl.ds(combo * slots * width + step, slots, stride=width), :]
        turned = block.T
        north.append(turned[:half])
        south.append(turned[half:])
    first = jnp.concatenate(north, 0).astype(jnp.bfloat16)
    second = jnp.concatenate(south, 0).astype(jnp.bfloat16)
    basis = legendre[0]
    ordered = dot(first, select[0]) + dot(second, select[1])
    latitude = lax.broadcasted_iota(jnp.int32, (1, lat_count), 1)
    keep = latitude >= LBLK * trim
    ordered = jnp.where(keep, ordered, 0.0).astype(jnp.bfloat16)
    coeffs = dot(ordered, basis)
    row = lax.broadcasted_iota(jnp.int32, (1, row_count), 1)
    degree = (row + wavenum).astype(jnp.float32)
    factor = degree * (degree + 1.0) * (1.0 / float(row_count * (row_count - 1)))
    south_side = lax.broadcasted_iota(jnp.int32, (coeffs.shape[0], 1), 0) % 2
    flip = (south_side * (row % 2)) == 1
    coeffs = jnp.where(flip, -coeffs, coeffs).astype(jnp.bfloat16)
    modal = dot(into[...], coeffs)
    scaled = (modal / (1.0 + factor * implicit[...])).astype(jnp.bfloat16)
    solved = dot(back[...], scaled)
    solved = jnp.where(row + wavenum < row_count, solved, 0.0)
    solved = jnp.where(flip, -solved, solved).astype(jnp.bfloat16)
    sides = dot(solved, basis, NT)
    sides = jnp.where(keep, sides, 0.0).astype(jnp.bfloat16)
    first = dot(sides, select[0], NT)
    second = dot(sides, select[1], NT)
    for combo in range(2 * levels):
        span = slice(combo * half, (combo + 1) * half)
        block = jnp.concatenate([first[span], second[span]], 0).T
        made[pl.ds(combo * slots * width + step, slots, stride=width), :] = block

    @pl.when(step == pl.num_programs(0) - 1)
    def _():
        for owner in range(owners):
            group, level = owner // levels, owner % levels
            for part in range(2):
                first = ((level * 2 + part) * groups + group) * count
                block = made[pl.ds(first * width, count * width), :]
                out[owner, part] = block.reshape(count, width, LANES).astype(jnp.bfloat16)


def middle(data, meta, legendre, select, into, back, implicit, levels):
    owners, _, count, width, _ = data.shape
    whole = lambda a: pl.BlockSpec(a.shape, lambda i, _: (0,) * a.ndim)
    rows = owners * 2 * count * width
    return pl.pallas_call(
        functools.partial(middle_kernel, levels=levels),
        grid_spec=pltpu.PrefetchScalarGridSpec(
            num_scalar_prefetch=1,
            grid=(width,),
            in_specs=[
                whole(data),
                pl.BlockSpec((1,) + legendre.shape[1:], lambda i, meta: (meta[2, i], 0, 0)),
                whole(select),
                whole(into),
                whole(back),
                whole(implicit),
            ],
            out_specs=whole(data),
            scratch_shapes=[pltpu.VMEM((rows, LANES), jnp.float32)] * 2,
        ),
        out_shape=jax.ShapeDtypeStruct(data.shape, jnp.bfloat16),
        name="middle",
    )(meta, data, legendre, select, into, back, implicit)


def place_kernel(*refs, count, final, with_start, split):
    blocks, targets = refs[:count], refs[count : 2 * count]
    refs = refs[2 * count :]
    start = refs[0] if with_start else None
    out = refs[1] if with_start else refs[0]
    tables = refs[-count:]

    @pl.when(pl.program_id(0) == 0)
    def _():
        for target, table in zip(targets, tables):
            column = lax.broadcasted_iota(jnp.int32, table.shape, 1)
            per = table.shape[0] // split
            goal = target[...]
            for piece in range(split):
                span = slice(piece * per, (piece + 1) * per)
                wanted = goal[span] - piece * table.shape[1]
                table[span, :] = jnp.where(column[span] == wanted, 1.0, 0.0).astype(jnp.bfloat16)

    turned = []
    for block in blocks:
        rows = block[:, :, 0].astype(jnp.float32).reshape(-1, LANES)
        turned.append(rows.T.astype(jnp.bfloat16))
    pieces = []
    for piece in range(split):
        total = None
        for rows, table in zip(turned, tables):
            per = table.shape[0] // split
            span = slice(piece * per, (piece + 1) * per)
            part = dot(rows[:, span], table[span, :])
            total = part if total is None else total + part
        pieces.append(total)
    placed = jnp.concatenate(pieces, 1) if split > 1 else pieces[0]
    if with_start:
        placed = placed + start[...].astype(jnp.float32)
    placed = placed.astype(jnp.bfloat16)
    if not final:
        out[...] = placed
        return
    low, fields = out.shape[1], out.shape[0]
    per = 2 * fields
    for slot in range(low):
        block = placed[slot * per : (slot + 1) * per]
        out[:, slot] = block.reshape(fields, 2, block.shape[1])


def place(blocks, targets, start, columns, fields, low, final):
    owners, _, count, _, _ = blocks[0].shape
    split = 2 if owners % 2 == 0 and (columns // 2) % LANES == 0 else 1
    specs = [
        pl.BlockSpec((owners, 2, 1) + b.shape[3:], lambda i: (0, 0, i, 0, 0)) for b in blocks
    ]
    specs += [pl.BlockSpec(t.shape, lambda i: (0, 0)) for t in targets]
    args = list(blocks) + list(targets)
    if start is not None:
        specs.append(pl.BlockSpec((LANES, columns), lambda i: (i, 0)))
        args.append(start)
    if final:
        out_spec = pl.BlockSpec((fields, low, 2, columns), lambda i: (0, i, 0, 0))
        out_shape = jax.ShapeDtypeStruct((fields, low * count, 2, columns), jnp.bfloat16)
    else:
        out_spec = pl.BlockSpec((LANES, columns), lambda i: (i, 0))
        out_shape = jax.ShapeDtypeStruct((LANES * count, columns), jnp.bfloat16)
    return pl.pallas_call(
        functools.partial(
            place_kernel, count=len(blocks), final=final, with_start=start is not None, split=split
        ),
        grid=(count,),
        in_specs=specs,
        out_specs=out_spec,
        out_shape=out_shape,
        scratch_shapes=[
            pltpu.VMEM((t.shape[0], columns // split), jnp.bfloat16) for t in targets
        ],
        name="place",
    )(*args)


def chunk_widths(tiles):
    if tiles < 3:
        return [TILE] * tiles
    return [TILE, (tiles - 2) * TILE, TILE]


def local(grid, lat_order, wave_order, trim, legendre, modes_in, modes_out, implicit):
    fields, lats, _, lon_count = grid.shape
    per_device, row_count, lat_count = legendre.shape
    levels = lax.axis_size("lev")
    groups = lax.axis_size("wave")
    owners = groups * levels
    low = LANES // (2 * fields)
    count = lats // low
    share = per_device // levels
    tiles = -(-share // TILE)
    widths = chunk_widths(tiles)

    me = lax.axis_index("wave") * levels + lax.axis_index("lev")
    slot = jnp.arange(tiles * TILE, dtype=jnp.int32)
    inside = jnp.minimum(slot, share - 1)
    owner_waves = wave_order.reshape(owners, share)[:, inside]
    my_waves = lax.dynamic_slice_in_dim(owner_waves, me, 1)[0]
    my_index = lax.axis_index("lev") * share + inside
    meta = jnp.stack([my_waves, trim[my_waves], my_index])
    first_column = jnp.arange(owners, dtype=jnp.int32)[:, None] * (2 * share)
    columns = jnp.where(slot < share, first_column + 2 * slot, -4 * per_device * owners)

    freqs, metas, targets, first = [], [], [], 0
    for width in widths:
        span = slice(first, first + width)
        waves = jnp.broadcast_to(owner_waves[:, None, span], (owners, 2, width))
        freqs.append(waves.reshape(-1, 1).astype(jnp.float32))
        goal = columns[:, None, span] + jnp.arange(2, dtype=jnp.int32)[None, :, None]
        targets.append(goal.reshape(-1, 1))
        metas.append(meta[:, span])
        first += width

    sent = dft(grid, freqs[:1], widths[:1], owners, low)
    if len(widths) > 1:
        sent += dft(grid, freqs[1:], widths[1:], owners, low)

    slots = lat_order.reshape(groups * count, low).T
    select = (slots[:, :, None] == jnp.arange(lat_count, dtype=jnp.int32)).astype(jnp.bfloat16)
    same = jnp.eye(2, dtype=jnp.bfloat16)
    split_in = modes_in.reshape(-1, levels, fields)
    into = jnp.einsum("klf,cd->ckldf", split_in, same)
    into = jnp.repeat(into.reshape(2 * levels * fields, 2 * levels * fields), 2, axis=1)
    split_out = modes_out.reshape(levels, fields, -1)
    back = jnp.einsum("lfk,cd->lcfdk", split_out, same)
    back = jnp.repeat(back.reshape(2 * levels * fields, 2 * levels * fields), 2, axis=0)
    tall = jnp.concatenate([implicit, implicit])[:, None]
    turned = jnp.swapaxes(legendre, 1, 2)

    exchange = functools.partial(
        lax.all_to_all, axis_name=AXES, split_axis=0, concat_axis=0, tiled=True
    )
    returned = []
    received = [exchange(block) for block in sent]
    for block, chunk in zip(received, metas):
        made = middle(block, chunk, turned, select, into, back, tall, levels)
        returned.append(exchange(made))
    start = None
    if len(widths) > 1:
        start = place(returned[:-1], targets[:-1], None, lon_count, fields, low, False)
    return place(returned[-1:], targets[-1:], start, lon_count, fields, low, True)


def solution(mesh):
    in_specs = (
        P(("member", "lev"), "wave", None, None),
        P(),
        P(),
        P(),
        P("wave", None, None),
        P(),
        P(),
        P(),
    )
    out_specs = P(("member", "lev"), "wave", None, None)
    return jax.shard_map(local, mesh=mesh, in_specs=in_specs, out_specs=out_specs, check_vma=False)
```

```python
import functools
import math

import jax
import jax.numpy as jnp
from jax import lax
from jax.experimental import pallas as pl
from jax.experimental.pallas import tpu as pltpu
from jax.sharding import PartitionSpec as P


LBLK = 64
LANES = 128
TILE = 8
AXES = ("wave", "lev")
NT = (((1,), (1,)), ((), ()))
NN = (((1,), (0,)), ((), ()))


def dot(a, b, dims=NN):
    return lax.dot_general(a, b, dims, preferred_element_type=jnp.float32)


def cosine_rows(freq_ref, first, count, width, lon_count):
    freq = freq_ref[pl.ds(first, count), :]
    row = lax.broadcasted_iota(jnp.int32, (count, 1), 0) + first
    phase = ((row // width) % 2).astype(jnp.float32) * (lon_count // 4)
    longitude = lax.broadcasted_iota(jnp.int32, (count, lon_count), 1).astype(jnp.float32)
    turns = freq * longitude + phase
    whole = jnp.floor(turns * (1.0 / lon_count) + 0.5)
    rest = jnp.abs(turns - whole * lon_count) * (1.0 / lon_count)
    angle = (0.25 - rest) * (2.0 * math.pi)
    square = angle * angle
    value = jnp.full_like(square, -1.0 / 39916800.0)
    for term in (1.0 / 362880.0, -1.0 / 5040.0, 1.0 / 120.0, -1.0 / 6.0, 1.0):
        value = value * square + term
    return (value * angle * (1.0 / math.sqrt(lon_count))).astype(jnp.bfloat16)


def dft_kernel(grid_ref, freq, *refs, width, low, pairs):
    outs, table = refs[:-1], refs[-1]
    fields, lon_count = grid_ref.shape[0], grid_ref.shape[3]

    @pl.when(pl.program_id(0) == 0)
    def _():
        step = 2 * width

        @pl.loop(0, table.shape[0] // step)
        def _(i):
            first = pl.multiple_of(i * step, step)
            table[pl.ds(first, step), :] = cosine_rows(freq, first, step, width, lon_count)

    rows = [grid_ref[:, slot].reshape(2 * fields, lon_count) for slot in range(pairs * low)]
    spectra = dot(table[...], jnp.concatenate(rows, 0), NT)
    for pair in range(pairs):
        part = spectra[:, pair * LANES : (pair + 1) * LANES]
        part = part.reshape(-1, 2, width, LANES).astype(jnp.bfloat16)
        if len(outs) == 1:
            outs[0][:, :, pair] = part
        else:
            for piece, out in enumerate(outs):
                out[0, :, pair] = part[piece]


def dft(grid, freq, width, owners, low, separate):
    fields, lats, _, lon_count = grid.shape
    count = lats // low
    pairs = 2 if count % 2 == 0 else 1
    pieces, each = (owners, 1) if separate else (1, owners)
    return pl.pallas_call(
        functools.partial(dft_kernel, width=width, low=low, pairs=pairs),
        grid=(count // pairs,),
        in_specs=[
            pl.BlockSpec((fields, pairs * low, 2, lon_count), lambda i: (0, i, 0, 0)),
            pl.BlockSpec(freq.shape, lambda i: (0, 0)),
        ],
        out_specs=[pl.BlockSpec((each, 2, pairs, width, LANES), lambda i: (0, 0, i, 0, 0))]
        * pieces,
        out_shape=[jax.ShapeDtypeStruct((each, 2, count, width, LANES), jnp.bfloat16)] * pieces,
        scratch_shapes=[pltpu.VMEM((freq.shape[0], lon_count), jnp.bfloat16)],
        name="dft",
    )(grid, freq)


def middle_kernel(meta, peers, *refs, levels, pieces):
    data, refs = refs[:pieces], refs[pieces:]
    legendre, select, into, back, implicit = refs[:5]
    out, (held, made) = refs[5 : 5 + pieces], refs[5 + pieces :]
    step = pl.program_id(0)
    each, _, count, width, _ = data[0].shape
    owners = each * pieces
    groups = owners // levels
    half = LANES // 2
    lat_count, row_count = legendre.shape[1], legendre.shape[2]

    def place_of(owner, part):
        first = ((owner % levels) * 2 + part) * groups + owner // levels
        return pl.ds(pl.multiple_of(first * (count * width), TILE), count * width)

    @pl.when(step == 0)
    def _():
        for piece in range(owners):
            for part in range(2):
                block = data[piece // each][piece % each, part].astype(jnp.float32)
                held[place_of(peers[0, piece], part), :] = block.reshape(-1, LANES)

    wavenum, trim = meta[0, step], meta[1, step]
    slots = groups * count
    north, south = [], []
    for combo in range(2 * levels):
        block = held[pl.ds(combo * slots * width + step, slots, stride=width), :]
        turned = block.T
        north.append(turned[:half])
        south.append(turned[half:])
    first = jnp.concatenate(north, 0).astype(jnp.bfloat16)
    second = jnp.concatenate(south, 0).astype(jnp.bfloat16)
    basis = legendre[0]
    ordered = dot(first, select[0]) + dot(second, select[1])
    latitude = lax.broadcasted_iota(jnp.int32, (1, lat_count), 1)
    keep = latitude >= LBLK * trim
    ordered = jnp.where(keep, ordered, 0.0).astype(jnp.bfloat16)
    coeffs = dot(ordered, basis)
    row = lax.broadcasted_iota(jnp.int32, (1, row_count), 1)
    degree = (row + wavenum).astype(jnp.float32)
    factor = degree * (degree + 1.0) * (1.0 / float(row_count * (row_count - 1)))
    south_side = lax.broadcasted_iota(jnp.int32, (coeffs.shape[0], 1), 0) % 2
    flip = (south_side * (row % 2)) == 1
    coeffs = jnp.where(flip, -coeffs, coeffs).astype(jnp.bfloat16)
    modal = dot(into[...], coeffs)
    scaled = (modal / (1.0 + factor * implicit[...])).astype(jnp.bfloat16)
    solved = dot(back[...], scaled)
    solved = jnp.where(row + wavenum < row_count, solved, 0.0)
    solved = jnp.where(flip, -solved, solved).astype(jnp.bfloat16)
    sides = dot(solved, basis, NT)
    sides = jnp.where(keep, sides, 0.0).astype(jnp.bfloat16)
    first = dot(sides, select[0], NT)
    second = dot(sides, select[1], NT)
    for combo in range(2 * levels):
        span = slice(combo * half, (combo + 1) * half)
        block = jnp.concatenate([first[span], second[span]], 0).T
        made[pl.ds(combo * slots * width + step, slots, stride=width), :] = block

    @pl.when(step == pl.num_programs(0) - 1)
    def _():
        for piece in range(owners):
            for part in range(2):
                block = made[place_of(peers[1, piece], part), :].reshape(count, width, LANES)
                out[piece // each][piece % each, part] = block.astype(jnp.bfloat16)


def middle(data, meta, peers, legendre, select, into, back, implicit, levels):
    each, _, count, width, _ = data[0].shape
    whole = lambda a: pl.BlockSpec(a.shape, lambda i, *_: (0,) * a.ndim)
    rows = each * len(data) * 2 * count * width
    return pl.pallas_call(
        functools.partial(middle_kernel, levels=levels, pieces=len(data)),
        grid_spec=pltpu.PrefetchScalarGridSpec(
            num_scalar_prefetch=2,
            grid=(width,),
            in_specs=[whole(a) for a in data]
            + [pl.BlockSpec((1,) + legendre.shape[1:], lambda i, meta, _: (meta[2, i], 0, 0))]
            + [whole(a) for a in (select, into, back, implicit)],
            out_specs=[whole(a) for a in data],
            scratch_shapes=[pltpu.VMEM((rows, LANES), jnp.float32)] * 2,
        ),
        out_shape=[jax.ShapeDtypeStruct(a.shape, jnp.bfloat16) for a in data],
        name="middle",
    )(meta, peers, *data, legendre, select, into, back, implicit)


def place_kernel(peers, *refs, pieces, final, with_start, split):
    blocks, refs = refs[:pieces], refs[pieces:]
    target, refs = refs[0], refs[1:]
    start = refs[0] if with_start else None
    out, table, gathered = refs[-3:]
    per = table.shape[0] // split

    @pl.when(pl.program_id(0) == 0)
    def _():
        column = lax.broadcasted_iota(jnp.int32, table.shape, 1)
        goal = target[...]
        for piece in range(split):
            span = slice(piece * per, (piece + 1) * per)
            wanted = goal[span] - piece * table.shape[1]
            table[span, :] = jnp.where(column[span] == wanted, 1.0, 0.0).astype(jnp.bfloat16)

    each, _, _, width, _ = blocks[0].shape
    for piece in range(each * pieces):
        first = pl.multiple_of(peers[0, piece] * (2 * width), TILE)
        block = blocks[piece // each][piece % each, :, 0].astype(jnp.float32)
        gathered[pl.ds(first, 2 * width), :] = block.reshape(2 * width, LANES)
    rows = gathered[...].T.astype(jnp.bfloat16)
    placed = []
    for piece in range(split):
        span = slice(piece * per, (piece + 1) * per)
        placed.append(dot(rows[:, span], table[span, :]))
    placed = jnp.concatenate(placed, 1) if split > 1 else placed[0]
    placed = placed.astype(jnp.bfloat16)
    if with_start:
        placed = placed + start[...]
    if not final:
        out[...] = placed
        return
    low, fields = out.shape[1], out.shape[0]
    for slot in range(low):
        block = placed[slot * 2 * fields : (slot + 1) * 2 * fields]
        out[:, slot] = block.reshape(fields, 2, block.shape[1])


def place(blocks, peers, target, start, columns, fields, low, final):
    each, _, count, width, _ = blocks[0].shape
    owners = each * len(blocks)
    split = 2 if owners % 2 == 0 and (columns // 2) % LANES == 0 else 1
    specs = [pl.BlockSpec((each, 2, 1, width, LANES), lambda i, _: (0, 0, i, 0, 0))] * len(blocks)
    specs.append(pl.BlockSpec(target.shape, lambda i, _: (0, 0)))
    args = list(blocks) + [target]
    if start is not None:
        specs.append(pl.BlockSpec((LANES, columns), lambda i, _: (i, 0)))
        args.append(start)
    if final:
        out_spec = pl.BlockSpec((fields, low, 2, columns), lambda i, _: (0, i, 0, 0))
        out_shape = jax.ShapeDtypeStruct((fields, low * count, 2, columns), jnp.bfloat16)
    else:
        out_spec = pl.BlockSpec((LANES, columns), lambda i, _: (i, 0))
        out_shape = jax.ShapeDtypeStruct((LANES * count, columns), jnp.bfloat16)
    return pl.pallas_call(
        functools.partial(
            place_kernel, pieces=len(blocks), final=final, with_start=start is not None, split=split
        ),
        grid_spec=pltpu.PrefetchScalarGridSpec(
            num_scalar_prefetch=1,
            grid=(count,),
            in_specs=specs,
            out_specs=out_spec,
            scratch_shapes=[
                pltpu.VMEM((target.shape[0], columns // split), jnp.bfloat16),
                pltpu.VMEM((owners * 2 * width, LANES), jnp.float32),
            ],
        ),
        out_shape=out_shape,
        name="place",
    )(peers, *args)


def chunk_widths(tiles):
    if tiles == 1:
        return [TILE]
    first = max(1, tiles * 2 // 5)
    return [first * TILE, (tiles - first) * TILE]


def partner(me, piece, groups, levels, back):
    fast = 2 * levels if groups % 2 == 0 else levels
    slow = groups * levels // fast
    far = piece // fast
    high = (me // fast + (slow - far if back else far)) % slow
    near = me % fast
    if fast & (fast - 1) == 0:
        low = near ^ (piece % fast)
    else:
        low = (near + (fast - piece % fast if back else piece % fast)) % fast
    return high * fast + low


def shift(pieces, groups, levels):
    owners = groups * levels
    moved = [pieces[0]]
    for piece in range(1, owners):
        pairs = [(i, partner(i, piece, groups, levels, False)) for i in range(owners)]
        moved.append(lax.ppermute(pieces[piece], AXES, pairs))
    return moved


def local(grid, lat_order, wave_order, trim, legendre, modes_in, modes_out, implicit):
    fields, lats, _, lon_count = grid.shape
    per_device, _, lat_count = legendre.shape
    levels = lax.axis_size("lev")
    groups = lax.axis_size("wave")
    owners = groups * levels
    low = LANES // (2 * fields)
    count = lats // low
    share = per_device // levels
    tiles = -(-share // TILE)
    widths = chunk_widths(tiles)

    me = lax.axis_index("wave") * levels + lax.axis_index("lev")
    slot = jnp.arange(tiles * TILE, dtype=jnp.int32)
    inside = jnp.minimum(slot, share - 1)
    owner_waves = wave_order.reshape(owners, share)[:, inside]
    my_waves = lax.dynamic_slice_in_dim(owner_waves, me, 1)[0]
    my_index = lax.axis_index("lev") * share + inside
    meta = jnp.stack([my_waves, trim[my_waves], my_index])
    first_column = jnp.arange(owners, dtype=jnp.int32)[:, None] * (2 * share)
    columns = jnp.where(slot < share, first_column + 2 * slot, -4 * per_device * owners)

    piece = jnp.arange(owners, dtype=jnp.int32)
    natural = jnp.stack([piece, piece])
    paired = jnp.stack(
        [partner(me, piece, groups, levels, back) for back in (True, False)]
    )
    peers = [natural, paired]

    freqs, metas, targets, first = [], [], [], 0
    for which, width in enumerate(widths):
        span = slice(first, first + width)
        waves = owner_waves[:, span] if which == 0 else owner_waves[paired[1]][:, span]
        waves = jnp.broadcast_to(waves[:, None], (owners, 2, width))
        freqs.append(waves.reshape(-1, 1).astype(jnp.float32))
        goal = columns[:, None, span] + jnp.arange(2, dtype=jnp.int32)[None, :, None]
        targets.append(goal.reshape(-1, 1))
        metas.append(meta[:, span])
        first += width

    sent = []
    for which, (freq, width) in enumerate(zip(freqs, widths)):
        sent.append(dft(grid, freq, width, owners, low, which > 0))

    slots = lat_order.reshape(groups * count, low).T
    select = (slots[:, :, None] == jnp.arange(lat_count, dtype=jnp.int32)).astype(jnp.bfloat16)
    same = jnp.eye(2, dtype=jnp.bfloat16)
    split_in = modes_in.reshape(-1, levels, fields)
    into = jnp.einsum("klf,cd->ckldf", split_in, same)
    into = jnp.repeat(into.reshape(2 * levels * fields, 2 * levels * fields), 2, axis=1)
    split_out = modes_out.reshape(levels, fields, -1)
    back = jnp.einsum("lfk,cd->lcfdk", split_out, same)
    back = jnp.repeat(back.reshape(2 * levels * fields, 2 * levels * fields), 2, axis=0)
    tall = jnp.concatenate([implicit, implicit])[:, None]
    turned = jnp.swapaxes(legendre, 1, 2)

    def exchange(blocks):
        if len(blocks) == 1:
            return [lax.all_to_all(blocks[0], AXES, split_axis=0, concat_axis=0, tiled=True)]
        return shift(blocks, groups, levels)

    received = []
    for blocks in sent:
        received.append(exchange(blocks))
    returned = []
    for blocks, chunk, who in zip(received, metas, peers):
        made = middle(blocks, chunk, who, turned, select, into, back, tall, levels)
        returned.append(exchange(made))
    result = None
    for which, blocks in enumerate(returned):
        final = which == len(returned) - 1
        result = place(
            blocks, peers[which], targets[which], result, lon_count, fields, low, final
        )
    return result


def solution(mesh):
    in_specs = (
        P(("member", "lev"), "wave", None, None),
        P(),
        P(),
        P(),
        P("wave", None, None),
        P(),
        P(),
        P(),
    )
    out_specs = P(("member", "lev"), "wave", None, None)
    return jax.shard_map(local, mesh=mesh, in_specs=in_specs, out_specs=out_specs, check_vma=False)
```

```python
import functools
import math

import jax
import jax.numpy as jnp
from jax import lax
from jax.experimental import pallas as pl
from jax.experimental.pallas import tpu as pltpu
from jax.sharding import PartitionSpec as P


LBLK = 64
LANES = 128
TILE = 8
AXES = ("wave", "lev")
NT = (((1,), (1,)), ((), ()))
NN = (((1,), (0,)), ((), ()))


def dot(a, b, dims=NN):
    return lax.dot_general(a, b, dims, preferred_element_type=jnp.float32)


def cosine_rows(freq_ref, first, count, lon_count):
    freq = freq_ref[pl.ds(first, count), :]
    row = lax.broadcasted_iota(jnp.int32, (count, 1), 0) + first
    phase = ((row // TILE) % 2).astype(jnp.float32) * (lon_count // 4)
    longitude = lax.broadcasted_iota(jnp.int32, (count, lon_count), 1).astype(jnp.float32)
    turns = freq * longitude + phase
    whole = jnp.floor(turns * (1.0 / lon_count) + 0.5)
    rest = jnp.abs(turns - whole * lon_count) * (1.0 / lon_count)
    angle = (0.25 - rest) * (2.0 * math.pi)
    square = angle * angle
    value = jnp.full_like(square, -1.0 / 39916800.0)
    for term in (1.0 / 362880.0, -1.0 / 5040.0, 1.0 / 120.0, -1.0 / 6.0, 1.0):
        value = value * square + term
    return (value * angle * (1.0 / math.sqrt(lon_count))).astype(jnp.bfloat16)


def units(depths):
    starts, first = [], 0
    for depth in depths:
        starts.append((first, first + depth))
        first += 2 * depth
    return starts, first


def dft_kernel(lats_ref, *refs, depths, pairs, slots):
    views, freq, outs, table = refs[:slots], refs[slots], refs[slots + 1 : -1], refs[-1]
    fields, lon_count = views[0].shape[0], views[0].shape[3]
    step = pl.program_id(0)

    @pl.when(step == 0)
    def _():
        rows = 4 * TILE if table.shape[0] % (4 * TILE) == 0 else 2 * TILE

        @pl.loop(0, table.shape[0] // rows)
        def _(i):
            first = pl.multiple_of(i * rows, rows)
            table[pl.ds(first, rows), :] = cosine_rows(freq, first, rows, lon_count)

    values = [view[:, 0].reshape(2 * fields, lon_count) for view in views]
    spectra = dot(table[...], jnp.concatenate(values, 0), NT)
    spectra = spectra.reshape(-1, len(depths), 2, TILE, pairs * LANES)
    starts, _ = units(depths)
    each = outs[0].shape[0]

    def store(tile, pair, where):
        for part in range(2):
            block = spectra[:, tile, part, :, pair * LANES : (pair + 1) * LANES]
            block = block.astype(jnp.bfloat16)
            for piece, out in enumerate(outs):
                out[:, starts[tile][part] + where] = block[piece * each : (piece + 1) * each]

    for pair in range(pairs):
        where = step * pairs + pair
        for tile, depth in enumerate(depths):
            pl.when(where < depth)(functools.partial(store, tile, pair, where))


def dft(grid, order, freq, depths, owners, low, separate):
    fields, lats, _, lon_count = grid.shape
    count = lats // low
    pairs = 2 if count % 2 == 0 else 1
    slots = pairs * low
    pieces, each = (owners, 1) if separate else (1, owners)
    shape = (each, units(depths)[1], TILE, LANES)

    def view(slot):
        return pl.BlockSpec(
            (fields, 1, 2, lon_count), lambda i, order: (0, order[i * slots + slot], 0, 0)
        )

    return pl.pallas_call(
        functools.partial(dft_kernel, depths=depths, pairs=pairs, slots=slots),
        grid_spec=pltpu.PrefetchScalarGridSpec(
            num_scalar_prefetch=1,
            grid=(count // pairs,),
            in_specs=[view(slot) for slot in range(slots)]
            + [pl.BlockSpec(freq.shape, lambda i, _: (0, 0))],
            out_specs=[pl.BlockSpec(shape, lambda i, _: (0, 0, 0, 0))] * pieces,
            scratch_shapes=[pltpu.VMEM((freq.shape[0], lon_count), jnp.bfloat16)],
        ),
        out_shape=[jax.ShapeDtypeStruct(shape, jnp.bfloat16)] * pieces,
        name="dft",
    )(order, *([grid] * slots), freq)


def middle_kernel(meta, peers, *refs, levels, pieces, depths, count):
    data, refs = refs[:pieces], refs[pieces:]
    legendre, select, into, back, implicit = refs[:5]
    out, (held, made) = refs[5 : 5 + pieces], refs[5 + pieces :]
    step = pl.program_id(0)
    each = data[0].shape[0]
    owners = each * pieces
    starts, _ = units(depths)
    groups = owners // levels
    half = LANES // 2
    lat_count, row_count = legendre.shape[1], legendre.shape[2]

    slots = groups * count
    tile_rows = 2 * levels * slots * TILE

    def place_of(owner, tile, part, first, rows):
        near = ((owner % levels) * 2 + part) * groups + owner // levels
        start = near * (count * TILE) + (tile * tile_rows + first * TILE)
        return pl.ds(pl.multiple_of(start, TILE), rows * TILE)

    @pl.when(step == 0)
    def _():
        for piece in range(owners):
            owner = peers[0, piece]
            for tile, depth in enumerate(depths):
                for part in range(2):
                    first = starts[tile][part]
                    block = data[piece // each][piece % each, first : first + depth]
                    block = block.astype(jnp.float32).reshape(-1, LANES)
                    held[place_of(owner, tile, part, 0, depth), :] = block
                    if depth < count:
                        rest = count - depth
                        empty = jnp.zeros((rest * TILE, LANES), jnp.float32)
                        held[place_of(owner, tile, part, depth, rest), :] = empty

    origin = (step // TILE) * tile_rows + step % TILE

    def column(combo):
        return pl.ds(origin + combo * slots * TILE, slots, stride=TILE)

    wavenum, trim = meta[0, step], meta[1, step]
    north, south = [], []
    for combo in range(2 * levels):
        block = held[column(combo), :]
        turned = block.T
        north.append(turned[:half])
        south.append(turned[half:])
    first = jnp.concatenate(north, 0).astype(jnp.bfloat16)
    second = jnp.concatenate(south, 0).astype(jnp.bfloat16)
    basis = legendre[0]
    ordered = dot(first, select[0]) + dot(second, select[1])
    latitude = lax.broadcasted_iota(jnp.int32, (1, lat_count), 1)
    keep = latitude >= LBLK * trim
    ordered = jnp.where(keep, ordered, 0.0).astype(jnp.bfloat16)
    coeffs = dot(ordered, basis)
    row = lax.broadcasted_iota(jnp.int32, (1, row_count), 1)
    degree = (row + wavenum).astype(jnp.float32)
    factor = degree * (degree + 1.0) * (1.0 / float(row_count * (row_count - 1)))
    south_side = lax.broadcasted_iota(jnp.int32, (coeffs.shape[0], 1), 0) % 2
    flip = (south_side * (row % 2)) == 1
    coeffs = jnp.where(flip, -coeffs, coeffs).astype(jnp.bfloat16)
    modal = dot(into[...], coeffs)
    scaled = (modal / (1.0 + factor * implicit[...])).astype(jnp.bfloat16)
    solved = dot(back[...], scaled)
    solved = jnp.where(row + wavenum < row_count, solved, 0.0)
    solved = jnp.where(flip, -solved, solved).astype(jnp.bfloat16)
    sides = dot(solved, basis, NT)
    sides = jnp.where(keep, sides, 0.0).astype(jnp.bfloat16)
    first = dot(sides, select[0], NT)
    second = dot(sides, select[1], NT)
    for combo in range(2 * levels):
        span = slice(combo * half, (combo + 1) * half)
        block = jnp.concatenate([first[span], second[span]], 0).T
        made[column(combo), :] = block

    @pl.when(step == pl.num_programs(0) - 1)
    def _():
        for piece in range(owners):
            owner = peers[1, piece]
            for tile, depth in enumerate(depths):
                for part in range(2):
                    first = starts[tile][part]
                    block = made[place_of(owner, tile, part, 0, depth), :]
                    block = block.reshape(depth, TILE, LANES).astype(jnp.bfloat16)
                    out[piece // each][piece % each, first : first + depth] = block


def middle(data, meta, peers, legendre, select, into, back, implicit, levels, depths, count):
    each = data[0].shape[0]
    whole = lambda a: pl.BlockSpec(a.shape, lambda i, *_: (0,) * a.ndim)
    rows = each * len(data) * 2 * count * TILE * len(depths)
    return pl.pallas_call(
        functools.partial(
            middle_kernel, levels=levels, pieces=len(data), depths=depths, count=count
        ),
        grid_spec=pltpu.PrefetchScalarGridSpec(
            num_scalar_prefetch=2,
            grid=(len(depths) * TILE,),
            in_specs=[whole(a) for a in data]
            + [pl.BlockSpec((1,) + legendre.shape[1:], lambda i, meta, _: (meta[2, i], 0, 0))]
            + [whole(a) for a in (select, into, back, implicit)],
            out_specs=[whole(a) for a in data],
            scratch_shapes=[pltpu.VMEM((rows, LANES), jnp.float32)] * 2,
        ),
        out_shape=[jax.ShapeDtypeStruct(a.shape, jnp.bfloat16) for a in data],
        name="middle",
    )(meta, peers, *data, legendre, select, into, back, implicit)


def place_kernel(peers, rank, *refs, pieces, final, with_start, split, depths, low, batch):
    blocks, refs = refs[:pieces], refs[pieces:]
    target, refs = refs[0], refs[1:]
    start = refs[0] if with_start else None
    out, table, gathered = refs[-3:]
    per = table.shape[0] // split
    each = blocks[0].shape[0]
    span_rows = 2 * TILE * len(depths)
    span = LANES // low
    starts, _ = units(depths)
    step = pl.program_id(0)

    @pl.when(step == 0)
    def _():
        column = lax.broadcasted_iota(jnp.int32, table.shape, 1)
        goal = target[...]
        for piece in range(split):
            rows = slice(piece * per, (piece + 1) * per)
            wanted = goal[rows] - piece * table.shape[1]
            table[rows, :] = jnp.where(column[rows] == wanted, 1.0, 0.0).astype(jnp.bfloat16)

    lane = lax.broadcasted_iota(jnp.int32, (1, LANES), 1) // span
    turned = []
    for item in range(batch):
        merged = None
        for slot in range(low):
            index = rank[(step * batch + item) * low + slot]
            where, side = index // low, index % low
            for piece in range(each * pieces):
                base = peers[0, piece] * span_rows
                for tile, depth in enumerate(depths):
                    near = jnp.minimum(where, depth - 1)
                    for part in range(2):
                        unit = starts[tile][part] + near
                        block = blocks[piece // each][piece % each, unit].astype(jnp.float32)
                        if depth < max_depth(rank, low):
                            block = jnp.where(where < depth, block, 0.0)
                        first = base + (2 * tile + part) * TILE
                        gathered[slot, pl.ds(pl.multiple_of(first, TILE), TILE), :] = block
            values = pltpu.roll(gathered[slot], ((slot - side) % low) * span, 1)
            merged = values if merged is None else jnp.where(lane == slot, values, merged)
        turned.append(merged.T.astype(jnp.bfloat16))
    rows = jnp.concatenate(turned, 0)
    placed = []
    for piece in range(split):
        part = slice(piece * per, (piece + 1) * per)
        placed.append(dot(rows[:, part], table[part, :]))
    placed = jnp.concatenate(placed, 1) if split > 1 else placed[0]
    placed = placed.astype(jnp.bfloat16)
    if with_start:
        placed = placed + start[...]
    if not final:
        out[...] = placed
        return
    fields = out.shape[0]
    for slot in range(batch * low):
        block = placed[slot * 2 * fields : (slot + 1) * 2 * fields]
        out[:, slot] = block.reshape(fields, 2, block.shape[1])


def max_depth(rank, low):
    return rank.shape[0] // low


def place(blocks, peers, rank, target, start, columns, fields, low, final, depths):
    each = blocks[0].shape[0]
    owners = each * len(blocks)
    count = rank.shape[0] // low
    batch = max(b for b in (1, 2, 4) if count % b == 0)
    split = 2 if owners % 2 == 0 and (columns // 2) % LANES == 0 else 1
    specs = [pl.BlockSpec(b.shape, lambda i, *_: (0, 0, 0, 0)) for b in blocks]
    specs.append(pl.BlockSpec(target.shape, lambda i, *_: (0, 0)))
    args = list(blocks) + [target]
    if start is not None:
        specs.append(pl.BlockSpec((batch * LANES, columns), lambda i, *_: (i, 0)))
        args.append(start)
    if final:
        out_spec = pl.BlockSpec((fields, low * batch, 2, columns), lambda i, *_: (0, i, 0, 0))
        out_shape = jax.ShapeDtypeStruct((fields, low * count, 2, columns), jnp.bfloat16)
    else:
        out_spec = pl.BlockSpec((batch * LANES, columns), lambda i, *_: (i, 0))
        out_shape = jax.ShapeDtypeStruct((LANES * count, columns), jnp.bfloat16)
    rows = target.shape[0]
    return pl.pallas_call(
        functools.partial(
            place_kernel,
            pieces=len(blocks),
            final=final,
            with_start=start is not None,
            split=split,
            depths=depths,
            low=low,
            batch=batch,
        ),
        grid_spec=pltpu.PrefetchScalarGridSpec(
            num_scalar_prefetch=2,
            grid=(count // batch,),
            in_specs=specs,
            out_specs=out_spec,
            scratch_shapes=[
                pltpu.VMEM((rows, columns // split), jnp.bfloat16),
                pltpu.VMEM((low, rows, LANES), jnp.float32),
            ],
        ),
        out_shape=out_shape,
        name="place",
    )(peers, rank, *args)


def chunk_tiles(tiles):
    first = max(1, tiles * 2 // 5)
    return [first, tiles - first] if tiles > first else [first]


def partner(me, piece, groups, levels, back):
    fast = 2 * levels if groups % 2 == 0 else levels
    slow = groups * levels // fast
    far = piece // fast
    high = (me // fast + (slow - far if back else far)) % slow
    near = me % fast
    if fast & (fast - 1) == 0:
        low = near ^ (piece % fast)
    else:
        low = (near + (fast - piece % fast if back else piece % fast)) % fast
    return high * fast + low


def shift(pieces, groups, levels):
    owners = groups * levels
    moved = [pieces[0]]
    for piece in range(1, owners):
        pairs = [(i, partner(i, piece, groups, levels, False)) for i in range(owners)]
        moved.append(lax.ppermute(pieces[piece], AXES, pairs))
    return moved


def ordered(keys):
    rank = jnp.sum((keys[:, None, :] < keys[:, :, None]).astype(jnp.int32), 2)
    spot = jnp.arange(keys.shape[1], dtype=jnp.int32)
    chosen = jnp.where(rank[:, :, None] == spot, keys[:, :, None], 0)
    return jnp.sum(chosen, 1), rank


def profiles(tiles, count):
    shares = [(0.4, 1.0), (0.6, 0.95), (0.8, 0.8), (1.0, 0.6)]
    small = []
    for tile in range(tiles):
        share = next(share for bound, share in shares if tile + 0.5 < bound * tiles)
        small.append(min(count, math.ceil(share * count - 1e-6)))
    return [small, [count] * tiles]


def local(grid, lat_order, wave_order, trim, legendre, modes_in, modes_out, implicit):
    fields, lats, _, lon_count = grid.shape
    per_device, row_count, lat_count = legendre.shape
    levels = lax.axis_size("lev")
    groups = lax.axis_size("wave")
    owners = groups * levels
    low = LANES // (2 * fields)
    count = lats // low
    share = per_device // levels
    tiles = -(-share // TILE)
    group = lax.axis_index("wave")
    me = group * levels + lax.axis_index("lev")

    trims = trim[wave_order].reshape(groups, per_device)
    near = jnp.arange(per_device, dtype=jnp.int32)
    keys = (trims * per_device + near) * row_count + wave_order.reshape(groups, per_device)
    keys, _ = ordered(keys)
    keys = keys.reshape(groups, share, levels).transpose(0, 2, 1).reshape(owners, share)
    slot = jnp.arange(tiles * TILE, dtype=jnp.int32)
    keys = keys[:, jnp.minimum(slot, share - 1)]
    owner_waves, owner_near = keys % row_count, keys // row_count % per_device
    owner_trims = keys // (row_count * per_device)
    table = (lat_count - 1 - lat_order).reshape(groups, lats)
    table, rank = ordered(table * lats + jnp.arange(lats, dtype=jnp.int32))
    slot_lats, slot_order = lat_count - 1 - table // lats, table % lats
    order = lax.dynamic_slice_in_dim(slot_order, group, 1)[0]
    rank = lax.dynamic_slice_in_dim(rank, group, 1)[0]

    mine = lax.dynamic_slice_in_dim(keys, me, 1)[0]
    meta = jnp.stack(
        [mine % row_count, mine // (row_count * per_device), mine // row_count % per_device]
    )
    first_column = (jnp.arange(owners, dtype=jnp.int32) // levels * (2 * per_device))[:, None]
    columns = jnp.where(slot < share, first_column + 2 * owner_near, -4 * per_device * owners)

    piece = jnp.arange(owners, dtype=jnp.int32)
    natural = jnp.stack([piece, piece])
    paired = jnp.stack(
        [partner(me, piece, groups, levels, back) for back in (True, False)]
    )
    peers = [natural, paired]

    freqs, metas, targets, spans, first = [], [], [], [], 0
    for which, size in enumerate(chunk_tiles(tiles)):
        spans.append(slice(first, first + size))
        span = slice(first * TILE, (first + size) * TILE)
        shape = (owners, size, 2, TILE)
        waves = owner_waves if which == 0 else owner_waves[paired[1]]
        waves = jnp.broadcast_to(waves[:, span].reshape(owners, size, 1, TILE), shape)
        freqs.append(waves.reshape(-1, 1).astype(jnp.float32))
        goal = columns[:, span].reshape(owners, size, 1, TILE)
        goal = goal + jnp.arange(2, dtype=jnp.int32)[:, None]
        targets.append(jnp.broadcast_to(goal, shape).reshape(-1, 1))
        metas.append(meta[:, span])
        first += size

    slots = slot_lats.reshape(groups * count, low).T
    select = (slots[:, :, None] == jnp.arange(lat_count, dtype=jnp.int32)).astype(jnp.bfloat16)
    same = jnp.eye(2, dtype=jnp.bfloat16)
    split_in = modes_in.reshape(-1, levels, fields)
    into = jnp.einsum("klf,cd->ckldf", split_in, same)
    into = jnp.repeat(into.reshape(2 * levels * fields, 2 * levels * fields), 2, axis=1)
    split_out = modes_out.reshape(levels, fields, -1)
    back = jnp.einsum("lfk,cd->lcfdk", split_out, same)
    back = jnp.repeat(back.reshape(2 * levels * fields, 2 * levels * fields), 2, axis=0)
    tall = jnp.concatenate([implicit, implicit])[:, None]
    turned = jnp.swapaxes(legendre, 1, 2)

    def exchange(blocks):
        if len(blocks) == 1:
            return [lax.all_to_all(blocks[0], AXES, split_axis=0, concat_axis=0, tiled=True)]
        return shift(blocks, groups, levels)

    def run(depths):
        depths = [tuple(depths[span]) for span in spans]
        sent = []
        for which, freq in enumerate(freqs):
            sent.append(dft(grid, order, freq, depths[which], owners, low, which > 0))
        received = []
        for blocks in sent:
            received.append(exchange(blocks))
        returned = []
        for which, blocks in enumerate(received):
            made = middle(
                blocks, metas[which], peers[which], turned, select, into, back, tall,
                levels, depths[which], count,
            )
            returned.append(exchange(made))
        result = None
        for which, blocks in enumerate(returned):
            final = which == len(returned) - 1
            result = place(
                blocks, peers[which], rank, targets[which], result, lon_count, fields, low,
                final, depths[which],
            )
        return result

    least = jnp.min(owner_trims[:, ::TILE], 0)
    needed = jnp.sum((slot_lats[:, None, :] >= LBLK * least[:, None]).astype(jnp.int32), 2)
    needed = jnp.max(needed, 0)
    choices = profiles(tiles, count)
    if PROFILE is not None:
        return run(choices[PROFILE])
    fits = jnp.all(needed <= low * jnp.array(choices[0], jnp.int32))
    return lax.cond(fits, lambda: run(choices[0]), lambda: run(choices[1]))


PROFILE = None


def solution(mesh):
    in_specs = (
        P(("member", "lev"), "wave", None, None),
        P(),
        P(),
        P(),
        P("wave", None, None),
        P(),
        P(),
        P(),
    )
    out_specs = P(("member", "lev"), "wave", None, None)
    return jax.shard_map(local, mesh=mesh, in_specs=in_specs, out_specs=out_specs, check_vma=False)
```

```python
import functools
import math

import jax
import jax.numpy as jnp
from jax import lax
from jax.experimental import pallas as pl
from jax.experimental.pallas import tpu as pltpu
from jax.sharding import PartitionSpec as P


LBLK = 64
LANES = 128
TILE = 8
AXES = ("wave", "lev")
NT = (((1,), (1,)), ((), ()))
NN = (((1,), (0,)), ((), ()))


def dot(a, b, dims=NN):
    return lax.dot_general(a, b, dims, preferred_element_type=jnp.float32)


def cosine_rows(freq_ref, first, count, lon_count):
    freq = freq_ref[pl.ds(first, count), :]
    row = lax.broadcasted_iota(jnp.int32, (count, 1), 0) + first
    phase = ((row // TILE) % 2).astype(jnp.float32) * (lon_count // 4)
    longitude = lax.broadcasted_iota(jnp.int32, (count, lon_count), 1).astype(jnp.float32)
    turns = freq * longitude + phase
    whole = jnp.floor(turns * (1.0 / lon_count) + 0.5)
    rest = jnp.abs(turns - whole * lon_count) * (1.0 / lon_count)
    angle = (0.25 - rest) * (2.0 * math.pi)
    square = angle * angle
    value = jnp.full_like(square, -1.0 / 39916800.0)
    for term in (1.0 / 362880.0, -1.0 / 5040.0, 1.0 / 120.0, -1.0 / 6.0, 1.0):
        value = value * square + term
    return (value * angle * (1.0 / math.sqrt(lon_count))).astype(jnp.bfloat16)


def units(depths):
    starts, first = [], 0
    for depth in depths:
        starts.append((first, first + depth))
        first += 2 * depth
    return starts, first


def dft_kernel(lats_ref, *refs, depths, pairs, slots):
    views, freq, outs, table = refs[:slots], refs[slots], refs[slots + 1 : -1], refs[-1]
    fields, lon_count = views[0].shape[0], views[0].shape[3]
    step = pl.program_id(0)

    @pl.when(step == 0)
    def _():
        rows = 4 * TILE if table.shape[0] % (4 * TILE) == 0 else 2 * TILE

        @pl.loop(0, table.shape[0] // rows)
        def _(i):
            first = pl.multiple_of(i * rows, rows)
            table[pl.ds(first, rows), :] = cosine_rows(freq, first, rows, lon_count)

    values = [view[:, 0].reshape(2 * fields, lon_count) for view in views]
    spectra = dot(table[...], jnp.concatenate(values, 0), NT)
    spectra = spectra.reshape(-1, len(depths), 2, TILE, pairs * LANES)
    starts, _ = units(depths)
    each = outs[0].shape[0]

    def store(tile, pair, where):
        for part in range(2):
            block = spectra[:, tile, part, :, pair * LANES : (pair + 1) * LANES]
            block = block.astype(jnp.bfloat16)
            for piece, out in enumerate(outs):
                out[:, starts[tile][part] + where] = block[piece * each : (piece + 1) * each]

    for pair in range(pairs):
        where = step * pairs + pair
        for tile, depth in enumerate(depths):
            pl.when(where < depth)(functools.partial(store, tile, pair, where))


def dft(grid, order, freq, depths, owners, lats, low, separate):
    fields, _, _, lon_count = grid.shape
    count = lats // low
    pairs = 2 if count % 2 == 0 else 1
    slots = pairs * low
    pieces, each = (owners, 1) if separate else (1, owners)
    shape = (each, units(depths)[1], TILE, LANES)

    def view(slot):
        return pl.BlockSpec(
            (fields, 1, 2, lon_count), lambda i, order: (0, order[0, i * slots + slot], 0, 0)
        )

    return pl.pallas_call(
        functools.partial(dft_kernel, depths=depths, pairs=pairs, slots=slots),
        grid_spec=pltpu.PrefetchScalarGridSpec(
            num_scalar_prefetch=1,
            grid=(count // pairs,),
            in_specs=[view(slot) for slot in range(slots)]
            + [pl.BlockSpec(freq.shape, lambda i, _: (0, 0))],
            out_specs=[pl.BlockSpec(shape, lambda i, _: (0, 0, 0, 0))] * pieces,
            scratch_shapes=[pltpu.VMEM((freq.shape[0], lon_count), jnp.bfloat16)],
        ),
        out_shape=[jax.ShapeDtypeStruct(shape, jnp.bfloat16)] * pieces,
        name="dft",
    )(order, *([grid] * slots), freq)


def as_column(row):
    return jnp.broadcast_to(row, (LANES, row.shape[1])).T[:, :1]


def plan_kernel(
    waves_ref, trim_ref, lats_ref, *outs, groups, levels, share, low, small, sizes, axes
):
    freqs, notes = outs[:-1], outs[-1]
    total = waves_ref.shape[1]
    near_count = total // groups
    waves = waves_ref[...].astype(jnp.float32)
    lane = lax.broadcasted_iota(jnp.int32, (1, total), 1).astype(jnp.float32)
    number = lax.broadcasted_iota(jnp.int32, (total, 1), 0).astype(jnp.float32)
    trim_column = as_column(trim_ref[...].astype(jnp.float32))
    trims = jnp.sum(jnp.where(number == waves, trim_column, 0.0), 0, keepdims=True)
    base = jnp.floor((lane + 0.5) * (1.0 / near_count)) * near_count
    keys = (base * 8.0 + trims * near_count) + (lane - base)
    rank = jnp.sum(jnp.where(as_column(keys) < keys, 1.0, 0.0), 0, keepdims=True)

    group = lax.axis_index(axes[0])
    me = group * levels + lax.axis_index(axes[1])
    first = 0
    for which, (freq, size) in enumerate(zip(freqs, sizes)):
        rows = size * 2 * TILE
        row = lax.broadcasted_iota(jnp.int32, (rows, 1), 0)
        tile, wave = row // (2 * TILE), row % TILE
        slot = jnp.minimum((first + tile) * TILE + wave, share - 1) * levels
        slot = slot.astype(jnp.float32)
        for piece in range(groups * levels):
            owner = jnp.int32(piece)
            if which > 0:
                owner = partner(me, jnp.int32(piece), groups, levels, False)
            start = ((owner // levels) * near_count + owner % levels).astype(jnp.float32)
            chosen = jnp.where(rank == slot + start, waves, 0.0)
            freq[piece * rows : (piece + 1) * rows, :] = jnp.sum(chosen, 1, keepdims=True)
        first += size

    lats = lats_ref[...]
    fits = jnp.full((1, 1), 1, jnp.int32)
    for tile, depth in enumerate(small):
        spot = (rank - base) == float(min(tile * TILE, share - 1) * levels)
        least = jnp.min(jnp.where(spot, trims, 8.0), 1, keepdims=True).astype(jnp.int32)
        needed = jnp.where(lats >= LBLK * least, 1.0, 0.0)
        needed = jnp.max(jnp.sum(needed, 1, keepdims=True), 0, keepdims=True)
        fits = fits * jnp.where(needed <= float(low * depth), 1, 0)

    count = lats.shape[1]
    mine = lats_ref[pl.ds(group, 1), :].astype(jnp.float32)
    mine = jnp.concatenate([mine, jnp.full((1, LANES - count), -1.0, jnp.float32)], 1)
    spot = lax.broadcasted_iota(jnp.int32, (1, LANES), 1).astype(jnp.float32)
    mine = mine * LANES - spot
    place_of = jnp.sum(jnp.where(as_column(mine) > mine, 1.0, 0.0), 0, keepdims=True)
    index = lax.broadcasted_iota(jnp.int32, (LANES, 1), 0).astype(jnp.float32)
    order = jnp.sum(jnp.where(as_column(place_of) == spot, index, 0.0), 0, keepdims=True)
    notes[0:1, :] = order.astype(jnp.int32)
    notes[1:2, :] = jnp.broadcast_to(fits, (1, LANES))


def plan(wave_order, trim, lat_order, groups, levels, share, low, small, sizes):
    total = wave_order.shape[0]
    owners = groups * levels
    return pl.pallas_call(
        functools.partial(
            plan_kernel, groups=groups, levels=levels, share=share, low=low, small=small,
            sizes=sizes, axes=AXES,
        ),
        out_shape=[
            jax.ShapeDtypeStruct((owners * size * 2 * TILE, 1), jnp.float32) for size in sizes
        ]
        + [jax.ShapeDtypeStruct((TILE, LANES), jnp.int32)],
        name="plan",
    )(wave_order.reshape(1, total), trim.reshape(1, total), lat_order.reshape(groups, -1))


def middle_kernel(meta, peers, *refs, levels, pieces, depths, count):
    data, refs = refs[:pieces], refs[pieces:]
    legendre, select, into, back, implicit = refs[:5]
    out, (held, made) = refs[5 : 5 + pieces], refs[5 + pieces :]
    step = pl.program_id(0)
    each = data[0].shape[0]
    owners = each * pieces
    starts, _ = units(depths)
    groups = owners // levels
    half = LANES // 2
    lat_count, row_count = legendre.shape[1], legendre.shape[2]

    slots = groups * count
    tile_rows = 2 * levels * slots * TILE

    def place_of(owner, tile, part, first, rows):
        near = ((owner % levels) * 2 + part) * groups + owner // levels
        start = near * (count * TILE) + (tile * tile_rows + first * TILE)
        return pl.ds(pl.multiple_of(start, TILE), rows * TILE)

    @pl.when(step == 0)
    def _():
        for piece in range(owners):
            owner = peers[0, piece]
            for tile, depth in enumerate(depths):
                for part in range(2):
                    first = starts[tile][part]
                    block = data[piece // each][piece % each, first : first + depth]
                    block = block.astype(jnp.float32).reshape(-1, LANES)
                    held[place_of(owner, tile, part, 0, depth), :] = block
                    if depth < count:
                        rest = count - depth
                        empty = jnp.zeros((rest * TILE, LANES), jnp.float32)
                        held[place_of(owner, tile, part, depth, rest), :] = empty

    origin = (step // TILE) * tile_rows + step % TILE

    def column(combo):
        return pl.ds(origin + combo * slots * TILE, slots, stride=TILE)

    wavenum, trim = meta[0, step], meta[1, step]
    north, south = [], []
    for combo in range(2 * levels):
        block = held[column(combo), :]
        turned = block.T
        north.append(turned[:half])
        south.append(turned[half:])
    first = jnp.concatenate(north, 0).astype(jnp.bfloat16)
    second = jnp.concatenate(south, 0).astype(jnp.bfloat16)
    basis = legendre[0]
    ordered = dot(first, select[0]) + dot(second, select[1])
    latitude = lax.broadcasted_iota(jnp.int32, (1, lat_count), 1)
    keep = latitude >= LBLK * trim
    ordered = jnp.where(keep, ordered, 0.0).astype(jnp.bfloat16)
    coeffs = dot(ordered, basis)
    row = lax.broadcasted_iota(jnp.int32, (1, row_count), 1)
    degree = (row + wavenum).astype(jnp.float32)
    factor = degree * (degree + 1.0) * (1.0 / float(row_count * (row_count - 1)))
    south_side = lax.broadcasted_iota(jnp.int32, (coeffs.shape[0], 1), 0) % 2
    flip = (south_side * (row % 2)) == 1
    coeffs = jnp.where(flip, -coeffs, coeffs).astype(jnp.bfloat16)
    modal = dot(into[...], coeffs)
    scaled = (modal / (1.0 + factor * implicit[...])).astype(jnp.bfloat16)
    solved = dot(back[...], scaled)
    solved = jnp.where(row + wavenum < row_count, solved, 0.0)
    solved = jnp.where(flip, -solved, solved).astype(jnp.bfloat16)
    sides = dot(solved, basis, NT)
    sides = jnp.where(keep, sides, 0.0).astype(jnp.bfloat16)
    first = dot(sides, select[0], NT)
    second = dot(sides, select[1], NT)
    for combo in range(2 * levels):
        span = slice(combo * half, (combo + 1) * half)
        block = jnp.concatenate([first[span], second[span]], 0).T
        made[column(combo), :] = block

    @pl.when(step == pl.num_programs(0) - 1)
    def _():
        for piece in range(owners):
            owner = peers[1, piece]
            for tile, depth in enumerate(depths):
                for part in range(2):
                    first = starts[tile][part]
                    block = made[place_of(owner, tile, part, 0, depth), :]
                    block = block.reshape(depth, TILE, LANES).astype(jnp.bfloat16)
                    out[piece // each][piece % each, first : first + depth] = block


def middle(data, meta, peers, legendre, select, into, back, implicit, levels, depths, count):
    each = data[0].shape[0]
    whole = lambda a: pl.BlockSpec(a.shape, lambda i, *_: (0,) * a.ndim)
    rows = each * len(data) * 2 * count * TILE * len(depths)
    return pl.pallas_call(
        functools.partial(
            middle_kernel, levels=levels, pieces=len(data), depths=depths, count=count
        ),
        grid_spec=pltpu.PrefetchScalarGridSpec(
            num_scalar_prefetch=2,
            grid=(len(depths) * TILE,),
            in_specs=[whole(a) for a in data]
            + [pl.BlockSpec((1,) + legendre.shape[1:], lambda i, meta, _: (meta[2, i], 0, 0))]
            + [whole(a) for a in (select, into, back, implicit)],
            out_specs=[whole(a) for a in data],
            scratch_shapes=[pltpu.VMEM((rows, LANES), jnp.float32)] * 2,
        ),
        out_shape=[jax.ShapeDtypeStruct(a.shape, jnp.bfloat16) for a in data],
        name="middle",
    )(meta, peers, *data, legendre, select, into, back, implicit)


def place_kernel(rank, *refs, pieces, final, with_start, split, depths, low, batch):
    blocks, refs = refs[:pieces], refs[pieces:]
    target, refs = refs[0], refs[1:]
    start = refs[0] if with_start else None
    out, table, gathered = refs[-3:]
    per = table.shape[0] // split
    each = blocks[0].shape[0]
    span_rows = 2 * TILE * len(depths)
    span = LANES // low
    starts, _ = units(depths)
    step = pl.program_id(0)

    @pl.when(step == 0)
    def _():
        column = lax.broadcasted_iota(jnp.int32, table.shape, 1)
        goal = target[...]
        for piece in range(split):
            rows = slice(piece * per, (piece + 1) * per)
            wanted = goal[rows] - piece * table.shape[1]
            table[rows, :] = jnp.where(column[rows] == wanted, 1.0, 0.0).astype(jnp.bfloat16)

    lane = lax.broadcasted_iota(jnp.int32, (1, LANES), 1) // span
    turned = []
    for item in range(batch):
        merged = None
        for slot in range(low):
            index = rank[(step * batch + item) * low + slot]
            where, side = index // low, index % low
            for piece in range(each * pieces):
                for tile, depth in enumerate(depths):
                    near = jnp.minimum(where, depth - 1)
                    for part in range(2):
                        unit = starts[tile][part] + near
                        block = blocks[piece // each][piece % each, unit].astype(jnp.float32)
                        if depth < rank.shape[0] // low:
                            block = jnp.where(where < depth, block, 0.0)
                        first = piece * span_rows + (2 * tile + part) * TILE
                        gathered[slot, first : first + TILE, :] = block
            values = pltpu.roll(gathered[slot], ((slot - side) % low) * span, 1)
            merged = values if merged is None else jnp.where(lane == slot, values, merged)
        turned.append(merged.T.astype(jnp.bfloat16))
    rows = jnp.concatenate(turned, 0)
    placed = []
    for piece in range(split):
        part = slice(piece * per, (piece + 1) * per)
        placed.append(dot(rows[:, part], table[part, :]))
    placed = jnp.concatenate(placed, 1) if split > 1 else placed[0]
    placed = placed.astype(jnp.bfloat16)
    if with_start:
        placed = placed + start[...]
    if not final:
        out[...] = placed
        return
    fields = out.shape[0]
    for slot in range(batch * low):
        block = placed[slot * 2 * fields : (slot + 1) * 2 * fields]
        out[:, slot] = block.reshape(fields, 2, block.shape[1])


def place(blocks, rank, target, start, columns, fields, low, final, depths):
    each = blocks[0].shape[0]
    owners = each * len(blocks)
    count = rank.shape[0] // low
    batch = max(b for b in (1, 2, 4) if count % b == 0)
    split = 2 if len(blocks) == 1 and owners % 2 == 0 and (columns // 2) % LANES == 0 else 1
    specs = [pl.BlockSpec(b.shape, lambda i, *_: (0, 0, 0, 0)) for b in blocks]
    specs.append(pl.BlockSpec(target.shape, lambda i, *_: (0, 0)))
    args = list(blocks) + [target]
    if start is not None:
        specs.append(pl.BlockSpec((batch * LANES, columns), lambda i, *_: (i, 0)))
        args.append(start)
    if final:
        out_spec = pl.BlockSpec((fields, low * batch, 2, columns), lambda i, *_: (0, i, 0, 0))
        out_shape = jax.ShapeDtypeStruct((fields, low * count, 2, columns), jnp.bfloat16)
    else:
        out_spec = pl.BlockSpec((batch * LANES, columns), lambda i, *_: (i, 0))
        out_shape = jax.ShapeDtypeStruct((LANES * count, columns), jnp.bfloat16)
    rows = target.shape[0]
    return pl.pallas_call(
        functools.partial(
            place_kernel,
            pieces=len(blocks),
            final=final,
            with_start=start is not None,
            split=split,
            depths=depths,
            low=low,
            batch=batch,
        ),
        grid_spec=pltpu.PrefetchScalarGridSpec(
            num_scalar_prefetch=1,
            grid=(count // batch,),
            in_specs=specs,
            out_specs=out_spec,
            scratch_shapes=[
                pltpu.VMEM((rows, columns // split), jnp.bfloat16),
                pltpu.VMEM((low, rows, LANES), jnp.float32),
            ],
        ),
        out_shape=out_shape,
        name="place",
    )(rank, *args)


def chunk_tiles(tiles):
    first = max(1, tiles * 2 // 5)
    return [first, tiles - first] if tiles > first else [first]


def partner(me, piece, groups, levels, back):
    fast = 2 * levels if groups % 2 == 0 else levels
    slow = groups * levels // fast
    far = piece // fast
    high = (me // fast + (slow - far if back else far)) % slow
    near = me % fast
    if fast & (fast - 1) == 0:
        low = near ^ (piece % fast)
    else:
        low = (near + (fast - piece % fast if back else piece % fast)) % fast
    return high * fast + low


def shift(pieces, groups, levels):
    owners = groups * levels
    moved = [pieces[0]]
    for piece in range(1, owners):
        pairs = [(i, partner(i, piece, groups, levels, False)) for i in range(owners)]
        moved.append(lax.ppermute(pieces[piece], AXES, pairs))
    return moved


def ordered(keys):
    rank = jnp.sum((keys[:, None, :] < keys[:, :, None]).astype(jnp.int32), 2)
    spot = jnp.arange(keys.shape[1], dtype=jnp.int32)
    chosen = jnp.where(rank[:, :, None] == spot, keys[:, :, None], 0)
    return jnp.sum(chosen, 1), rank


def profiles(tiles, count):
    shares = [(0.4, 1.0), (0.6, 0.95), (0.8, 0.8), (1.0, 0.6)]
    small = []
    for tile in range(tiles):
        share = next(share for bound, share in shares if tile + 0.5 < bound * tiles)
        small.append(min(count, math.ceil(share * count - 1e-6)))
    return [small, [count] * tiles]


def local(grid, lat_order, wave_order, trim, legendre, modes_in, modes_out, implicit):
    fields, lats, _, lon_count = grid.shape
    per_device, row_count, lat_count = legendre.shape
    levels = lax.axis_size("lev")
    groups = lax.axis_size("wave")
    owners = groups * levels
    low = LANES // (2 * fields)
    count = lats // low
    share = per_device // levels
    tiles = -(-share // TILE)
    group = lax.axis_index("wave")
    me = group * levels + lax.axis_index("lev")

    def tables():
        trims = trim[wave_order].reshape(groups, per_device)
        near = jnp.arange(per_device, dtype=jnp.int32)
        keys = (trims * per_device + near) * row_count + wave_order.reshape(groups, per_device)
        keys, _ = ordered(keys)
        keys = keys.reshape(groups, share, levels).transpose(0, 2, 1).reshape(owners, share)
        slot = jnp.arange(tiles * TILE, dtype=jnp.int32)
        keys = keys[:, jnp.minimum(slot, share - 1)]
        owner_near = keys // row_count % per_device
        table = (lat_count - 1 - lat_order).reshape(groups, lats)
        table, rank = ordered(table * lats + jnp.arange(lats, dtype=jnp.int32))
        slot_lats = lat_count - 1 - table // lats
        rank = lax.dynamic_slice_in_dim(rank, group, 1)[0]

        mine = lax.dynamic_slice_in_dim(keys, me, 1)[0]
        meta = jnp.stack(
            [mine % row_count, mine // (row_count * per_device), mine // row_count % per_device]
        )
        first_column = (jnp.arange(owners, dtype=jnp.int32) // levels * (2 * per_device))[:, None]
        columns = jnp.where(slot < share, first_column + 2 * owner_near, -4 * per_device * owners)

        piece = jnp.arange(owners, dtype=jnp.int32)
        natural = jnp.stack([piece, piece])
        paired = jnp.stack(
            [partner(me, piece, groups, levels, back) for back in (True, False)]
        )
        peers = [natural, paired]

        metas, targets, first = [], [], 0
        for which, size in enumerate(sizes):
            span = slice(first * TILE, (first + size) * TILE)
            shape = (owners, size, 2, TILE)
            goal = columns if which == 0 else columns[paired[0]]
            goal = goal[:, span].reshape(owners, size, 1, TILE)
            goal = goal + jnp.arange(2, dtype=jnp.int32)[:, None]
            targets.append(jnp.broadcast_to(goal, shape).reshape(-1, 1))
            metas.append(meta[:, span])
            first += size

        slots = slot_lats.reshape(groups * count, low).T
        select = (slots[:, :, None] == jnp.arange(lat_count, dtype=jnp.int32)).astype(jnp.bfloat16)
        same = jnp.eye(2, dtype=jnp.bfloat16)
        split_in = modes_in.reshape(-1, levels, fields)
        into = jnp.einsum("klf,cd->ckldf", split_in, same)
        into = jnp.repeat(into.reshape(2 * levels * fields, 2 * levels * fields), 2, axis=1)
        split_out = modes_out.reshape(levels, fields, -1)
        back = jnp.einsum("lfk,cd->lcfdk", split_out, same)
        back = jnp.repeat(back.reshape(2 * levels * fields, 2 * levels * fields), 2, axis=0)
        tall = jnp.concatenate([implicit, implicit])[:, None]
        turned = jnp.swapaxes(legendre, 1, 2)
        return metas, peers, rank, targets, (turned, select, into, back, tall)

    def exchange(blocks):
        if len(blocks) == 1:
            return [lax.all_to_all(blocks[0], AXES, split_axis=0, concat_axis=0, tiled=True)]
        return shift(blocks, groups, levels)

    def run(depths):
        depths = [tuple(depths[span]) for span in spans]
        sent = []
        for which, freq in enumerate(freqs):
            sent.append(dft(grid, notes, freq, depths[which], owners, lats, low, which > 0))
        metas, peers, rank, targets, weights = tables()
        received = []
        for blocks in sent:
            received.append(exchange(blocks))
        returned = []
        for which, blocks in enumerate(received):
            made = middle(
                blocks, metas[which], peers[which], *weights, levels, depths[which], count
            )
            returned.append(exchange(made))
        result = None
        for which, blocks in enumerate(returned):
            last = which == len(returned) - 1
            kept = len(blocks) * 3 // 4
            parts = [slice(0, kept), slice(kept, None)] if kept else [slice(0, None)]
            for part in parts:
                target = targets[which].reshape(len(blocks), -1)[part].reshape(-1, 1)
                result = place(
                    blocks[part], rank, target, result, lon_count, fields, low,
                    last and part is parts[-1], depths[which],
                )
        return result

    sizes = chunk_tiles(tiles)
    spans, first = [], 0
    for size in sizes:
        spans.append(slice(first, first + size))
        first += size
    small, full = profiles(tiles, count)
    *freqs, notes = plan(
        wave_order, trim, lat_order, groups, levels, share, low, small, sizes
    )
    if PROFILE is not None:
        return run((small, full)[PROFILE])
    return lax.cond(notes[1, 0] > 0, lambda: run(small), lambda: run(full))


PROFILE = None


def solution(mesh):
    in_specs = (
        P(("member", "lev"), "wave", None, None),
        P(),
        P(),
        P(),
        P("wave", None, None),
        P(),
        P(),
        P(),
    )
    out_specs = P(("member", "lev"), "wave", None, None)
    return jax.shard_map(local, mesh=mesh, in_specs=in_specs, out_specs=out_specs, check_vma=False)
```

```python
import functools
import math

import jax
import jax.numpy as jnp
from jax import lax
from jax.experimental import pallas as pl
from jax.experimental.pallas import tpu as pltpu
from jax.sharding import PartitionSpec as P


LBLK = 64
LANES = 128
TILE = 8
AXES = ("wave", "lev")
NT = (((1,), (1,)), ((), ()))
NN = (((1,), (0,)), ((), ()))


def dot(a, b, dims=NN):
    return lax.dot_general(a, b, dims, preferred_element_type=jnp.float32)


def cosine_rows(freq_ref, first, count, lon_count):
    freq = freq_ref[pl.ds(first, count), :]
    row = lax.broadcasted_iota(jnp.int32, (count, 1), 0) + first
    phase = ((row // TILE) % 2).astype(jnp.float32) * (lon_count // 4)
    longitude = lax.broadcasted_iota(jnp.int32, (count, lon_count), 1).astype(jnp.float32)
    turns = freq * longitude + phase
    whole = jnp.floor(turns * (1.0 / lon_count) + 0.5)
    rest = jnp.abs(turns - whole * lon_count) * (1.0 / lon_count)
    angle = (0.25 - rest) * (2.0 * math.pi)
    square = angle * angle
    value = jnp.full_like(square, -1.0 / 39916800.0)
    for term in (1.0 / 362880.0, -1.0 / 5040.0, 1.0 / 120.0, -1.0 / 6.0, 1.0):
        value = value * square + term
    return (value * angle * (1.0 / math.sqrt(lon_count))).astype(jnp.bfloat16)


def units(depths):
    starts, first = [], 0
    for depth in depths:
        starts.append((first, first + depth))
        first += 2 * depth
    return starts, first


def dft_kernel(lats_ref, *refs, depths, pairs, slots):
    views, freq, outs = refs[:slots], refs[slots], refs[slots + 1 : -3]
    table, halves = refs[-3], refs[-2:]
    fields, lon_count = views[0].shape[0], views[0].shape[3]
    step = pl.program_id(0)
    starts, _ = units(depths)
    each = outs[0].shape[0]

    def fill(half):
        for slot, view in enumerate(views):
            rows = slice(slot * 2 * fields, (slot + 1) * 2 * fields)
            half[rows, :] = view[:, 0].reshape(2 * fields, lon_count)

    @pl.when(step == 0)
    def _():
        rows = 4 * TILE if table.shape[0] % (4 * TILE) == 0 else 2 * TILE

        @pl.loop(0, table.shape[0] // rows)
        def _(i):
            first = pl.multiple_of(i * rows, rows)
            table[pl.ds(first, rows), :] = cosine_rows(freq, first, rows, lon_count)

        fill(halves[0])

    def store(spectra, tile, pair, where):
        for part in range(2):
            block = spectra[:, tile, part, :, pair * LANES : (pair + 1) * LANES]
            block = block.astype(jnp.bfloat16)
            for piece, out in enumerate(outs):
                out[:, starts[tile][part] + where] = block[piece * each : (piece + 1) * each]

    def advance(ready, later):
        spectra = dot(table[...], ready[...], NT)
        fill(later)
        spectra = spectra.reshape(-1, len(depths), 2, TILE, pairs * LANES)
        for pair in range(pairs):
            where = (step - 1) * pairs + pair
            for tile, depth in enumerate(depths):
                pl.when(where < depth)(functools.partial(store, spectra, tile, pair, where))

    odd = step % 2 == 1
    pl.when(odd)(functools.partial(advance, halves[0], halves[1]))
    even = (step > 0) & (step % 2 == 0)
    pl.when(even)(functools.partial(advance, halves[1], halves[0]))


def dft(grid, order, freq, depths, owners, lats, low, separate):
    fields, _, _, lon_count = grid.shape
    count = lats // low
    pairs = 2 if count % 2 == 0 else 1
    slots = pairs * low
    steps = count // pairs
    pieces, each = (owners, 1) if separate else (1, owners)
    shape = (each, units(depths)[1], TILE, LANES)

    def view(slot):
        return pl.BlockSpec(
            (fields, 1, 2, lon_count),
            lambda i, order: (0, order[0, jnp.minimum(i, steps - 1) * slots + slot], 0, 0),
        )

    return pl.pallas_call(
        functools.partial(dft_kernel, depths=depths, pairs=pairs, slots=slots),
        grid_spec=pltpu.PrefetchScalarGridSpec(
            num_scalar_prefetch=1,
            grid=(steps + 1,),
            in_specs=[view(slot) for slot in range(slots)]
            + [pl.BlockSpec(freq.shape, lambda i, _: (0, 0))],
            out_specs=[pl.BlockSpec(shape, lambda i, _: (0, 0, 0, 0))] * pieces,
            scratch_shapes=[pltpu.VMEM((freq.shape[0], lon_count), jnp.bfloat16)]
            + [pltpu.VMEM((pairs * LANES, lon_count), jnp.bfloat16)] * 2,
        ),
        out_shape=[jax.ShapeDtypeStruct(shape, jnp.bfloat16)] * pieces,
        name="dft",
    )(order, *([grid] * slots), freq)


def as_column(row):
    return jnp.broadcast_to(row, (LANES, row.shape[1])).T[:, :1]


def plan_kernel(
    waves_ref, trim_ref, lats_ref, *outs, groups, levels, share, low, small, sizes, axes
):
    freqs, notes = outs[:-1], outs[-1]
    total = waves_ref.shape[0]
    near_count = total // groups
    waves = waves_ref[...].reshape(1, -1).astype(jnp.float32)
    lane = lax.broadcasted_iota(jnp.int32, (1, total), 1).astype(jnp.float32)
    number = lax.broadcasted_iota(jnp.int32, (total, 1), 0).astype(jnp.float32)
    trim_column = as_column(trim_ref[...].reshape(1, -1).astype(jnp.float32))
    trims = jnp.sum(jnp.where(number == waves, trim_column, 0.0), 0, keepdims=True)
    base = jnp.floor((lane + 0.5) * (1.0 / near_count)) * near_count
    keys = (base * 8.0 + trims * near_count) + (lane - base)
    rank = jnp.sum(jnp.where(as_column(keys) < keys, 1.0, 0.0), 0, keepdims=True)

    group = lax.axis_index(axes[0])
    me = group * levels + lax.axis_index(axes[1])
    first = 0
    for which, (freq, size) in enumerate(zip(freqs, sizes)):
        rows = size * 2 * TILE
        row = lax.broadcasted_iota(jnp.int32, (rows, 1), 0)
        tile, wave = row // (2 * TILE), row % TILE
        slot = jnp.minimum((first + tile) * TILE + wave, share - 1) * levels
        slot = slot.astype(jnp.float32)
        for piece in range(groups * levels):
            owner = jnp.int32(piece)
            if which > 0:
                owner = partner(me, jnp.int32(piece), groups, levels, False)
            start = ((owner // levels) * near_count + owner % levels).astype(jnp.float32)
            chosen = jnp.where(rank == slot + start, waves, 0.0)
            freq[piece * rows : (piece + 1) * rows, :] = jnp.sum(chosen, 1, keepdims=True)
        first += size

    lats = lats_ref[...].reshape(1, -1).astype(jnp.float32)
    lat_count = lats.shape[1]
    slots = lat_count // groups
    lane = lax.broadcasted_iota(jnp.int32, (1, lat_count), 1).astype(jnp.float32)
    origin = jnp.floor((lane + 0.5) * (1.0 / slots)) * slots
    owner = lax.broadcasted_iota(jnp.int32, (groups, 1), 0).astype(jnp.float32) * slots == origin
    fits = jnp.full((1, 1), 1, jnp.int32)
    for tile, depth in enumerate(small):
        spot = (rank - base) == float(min(tile * TILE, share - 1) * levels)
        least = jnp.min(jnp.where(spot, trims, 8.0), 1, keepdims=True)
        needed = jnp.where(owner & (lats >= LBLK * least), 1.0, 0.0)
        needed = jnp.max(jnp.sum(needed, 1, keepdims=True), 0, keepdims=True)
        fits = fits * jnp.where(needed <= float(low * depth), 1, 0)

    keys = (origin + slots) * lat_count - lats
    place_of = jnp.sum(jnp.where(as_column(keys) < keys, 1.0, 0.0), 0, keepdims=True)
    spot = lax.broadcasted_iota(jnp.int32, (1, LANES), 1).astype(jnp.float32)
    start = (group * slots).astype(jnp.float32)
    index = lax.broadcasted_iota(jnp.int32, (lat_count, 1), 0).astype(jnp.float32) - start
    chosen = jnp.where(as_column(place_of) - start == spot, index, 0.0)
    order = jnp.sum(chosen, 0, keepdims=True)
    notes[0:1, :] = order.astype(jnp.int32)
    notes[1:2, :] = jnp.broadcast_to(fits, (1, LANES))


def plan(wave_order, trim, lat_order, groups, levels, share, low, small, sizes):
    owners = groups * levels
    return pl.pallas_call(
        functools.partial(
            plan_kernel, groups=groups, levels=levels, share=share, low=low, small=small,
            sizes=sizes, axes=AXES,
        ),
        out_shape=[
            jax.ShapeDtypeStruct((owners * size * 2 * TILE, 1), jnp.float32) for size in sizes
        ]
        + [jax.ShapeDtypeStruct((TILE, LANES), jnp.int32)],
        name="plan",
    )(wave_order, trim, lat_order)


def middle_kernel(meta, peers, *refs, levels, pieces, depths, count):
    data, refs = refs[:pieces], refs[pieces:]
    legendre, select, into, back, implicit = refs[:5]
    out, (held, made) = refs[5 : 5 + pieces], refs[5 + pieces :]
    step = pl.program_id(0)
    each = data[0].shape[0]
    owners = each * pieces
    starts, _ = units(depths)
    groups = owners // levels
    half = LANES // 2
    lat_count, row_count = legendre.shape[1], legendre.shape[2]

    slots = groups * count
    tile_rows = 2 * levels * slots * TILE

    def place_of(owner, tile, part, first, rows):
        near = ((owner % levels) * 2 + part) * groups + owner // levels
        start = near * (count * TILE) + (tile * tile_rows + first * TILE)
        return pl.ds(pl.multiple_of(start, TILE), rows * TILE)

    @pl.when(step == 0)
    def _():
        for piece in range(owners):
            owner = peers[0, piece]
            for tile, depth in enumerate(depths):
                for part in range(2):
                    first = starts[tile][part]
                    block = data[piece // each][piece % each, first : first + depth]
                    block = block.astype(jnp.float32).reshape(-1, LANES)
                    held[place_of(owner, tile, part, 0, depth), :] = block
                    if depth < count:
                        rest = count - depth
                        empty = jnp.zeros((rest * TILE, LANES), jnp.float32)
                        held[place_of(owner, tile, part, depth, rest), :] = empty

    origin = (step // TILE) * tile_rows + step % TILE

    def column(combo):
        return pl.ds(origin + combo * slots * TILE, slots, stride=TILE)

    wavenum, trim = meta[0, step], meta[1, step]
    north, south = [], []
    for combo in range(2 * levels):
        block = held[column(combo), :]
        turned = block.T
        north.append(turned[:half])
        south.append(turned[half:])
    first = jnp.concatenate(north, 0).astype(jnp.bfloat16)
    second = jnp.concatenate(south, 0).astype(jnp.bfloat16)
    basis = legendre[0]
    ordered = dot(first, select[0]) + dot(second, select[1])
    latitude = lax.broadcasted_iota(jnp.int32, (1, lat_count), 1)
    keep = latitude >= LBLK * trim
    ordered = jnp.where(keep, ordered, 0.0).astype(jnp.bfloat16)
    coeffs = dot(ordered, basis)
    row = lax.broadcasted_iota(jnp.int32, (1, row_count), 1)
    degree = (row + wavenum).astype(jnp.float32)
    factor = degree * (degree + 1.0) * (1.0 / float(row_count * (row_count - 1)))
    south_side = lax.broadcasted_iota(jnp.int32, (coeffs.shape[0], 1), 0) % 2
    flip = (south_side * (row % 2)) == 1
    coeffs = jnp.where(flip, -coeffs, coeffs).astype(jnp.bfloat16)
    modal = dot(into[...], coeffs)
    scaled = (modal / (1.0 + factor * implicit[...])).astype(jnp.bfloat16)
    solved = dot(back[...], scaled)
    solved = jnp.where(row + wavenum < row_count, solved, 0.0)
    solved = jnp.where(flip, -solved, solved).astype(jnp.bfloat16)
    sides = dot(solved, basis, NT)
    sides = jnp.where(keep, sides, 0.0).astype(jnp.bfloat16)
    first = dot(sides, select[0], NT)
    second = dot(sides, select[1], NT)
    for combo in range(2 * levels):
        span = slice(combo * half, (combo + 1) * half)
        block = jnp.concatenate([first[span], second[span]], 0).T
        made[column(combo), :] = block

    @pl.when(step == pl.num_programs(0) - 1)
    def _():
        for piece in range(owners):
            owner = peers[1, piece]
            for tile, depth in enumerate(depths):
                for part in range(2):
                    first = starts[tile][part]
                    block = made[place_of(owner, tile, part, 0, depth), :]
                    block = block.reshape(depth, TILE, LANES).astype(jnp.bfloat16)
                    out[piece // each][piece % each, first : first + depth] = block


def middle(data, meta, peers, legendre, select, into, back, implicit, levels, depths, count):
    each = data[0].shape[0]
    whole = lambda a: pl.BlockSpec(a.shape, lambda i, *_: (0,) * a.ndim)
    rows = each * len(data) * 2 * count * TILE * len(depths)
    return pl.pallas_call(
        functools.partial(
            middle_kernel, levels=levels, pieces=len(data), depths=depths, count=count
        ),
        grid_spec=pltpu.PrefetchScalarGridSpec(
            num_scalar_prefetch=2,
            grid=(len(depths) * TILE,),
            in_specs=[whole(a) for a in data]
            + [pl.BlockSpec((1,) + legendre.shape[1:], lambda i, meta, _: (meta[2, i], 0, 0))]
            + [whole(a) for a in (select, into, back, implicit)],
            out_specs=[whole(a) for a in data],
            scratch_shapes=[pltpu.VMEM((rows, LANES), jnp.float32)] * 2,
        ),
        out_shape=[jax.ShapeDtypeStruct(a.shape, jnp.bfloat16) for a in data],
        name="middle",
    )(meta, peers, *data, legendre, select, into, back, implicit)


def place_kernel(rank, *refs, pieces, final, with_start, split, depths, low, batch):
    blocks, refs = refs[:pieces], refs[pieces:]
    target, refs = refs[0], refs[1:]
    start = refs[0] if with_start else None
    out, table, gathered, held = refs[-4:]
    per = table.shape[0] // split
    each = blocks[0].shape[0]
    span_rows = 2 * TILE * len(depths)
    span = LANES // low
    starts, _ = units(depths)
    step = pl.program_id(0)

    @pl.when(step == 0)
    def _():
        column = lax.broadcasted_iota(jnp.int32, table.shape, 1)
        goal = target[...]
        for piece in range(split):
            rows = slice(piece * per, (piece + 1) * per)
            wanted = goal[rows] - piece * table.shape[1]
            table[rows, :] = jnp.where(column[rows] == wanted, 1.0, 0.0).astype(jnp.bfloat16)

    lane = lax.broadcasted_iota(jnp.int32, (1, LANES), 1) // span

    def turn(item):
        merged = None
        for slot in range(low):
            index = rank[(step * batch + item) * low + slot]
            where, side = index // low, index % low
            for piece in range(each * pieces):
                for tile, depth in enumerate(depths):
                    near = jnp.minimum(where, depth - 1)
                    for part in range(2):
                        unit = starts[tile][part] + near
                        block = blocks[piece // each][piece % each, unit].astype(jnp.float32)
                        if depth < rank.shape[0] // low:
                            block = jnp.where(where < depth, block, 0.0)
                        first = piece * span_rows + (2 * tile + part) * TILE
                        gathered[slot, first : first + TILE, :] = block
            values = pltpu.roll(gathered[slot], ((slot - side) % low) * span, 1)
            merged = values if merged is None else jnp.where(lane == slot, values, merged)
        return merged.T.astype(jnp.bfloat16)

    if final:
        rows = jnp.concatenate([turn(item) for item in range(batch)], 0)
    else:

        @pl.loop(0, batch)
        def _(item):
            held[pl.ds(pl.multiple_of(item * LANES, LANES), LANES), :] = turn(item)

        rows = held[...]
    placed = []
    for piece in range(split):
        part = slice(piece * per, (piece + 1) * per)
        placed.append(dot(rows[:, part], table[part, :]))
    placed = jnp.concatenate(placed, 1) if split > 1 else placed[0]
    placed = placed.astype(jnp.bfloat16)
    if with_start:
        placed = placed + start[...]
    if not final:
        out[...] = placed
        return
    fields = out.shape[0]
    for slot in range(batch * low):
        block = placed[slot * 2 * fields : (slot + 1) * 2 * fields]
        out[:, slot] = block.reshape(fields, 2, block.shape[1])


def place(blocks, rank, target, start, columns, fields, low, final, depths):
    each = blocks[0].shape[0]
    owners = each * len(blocks)
    count = rank.shape[0] // low
    batch = max(b for b in (1, 2, 4) if count % b == 0)
    split = 2 if len(blocks) == 1 and owners % 2 == 0 and (columns // 2) % LANES == 0 else 1
    specs = [pl.BlockSpec(b.shape, lambda i, *_: (0, 0, 0, 0)) for b in blocks]
    specs.append(pl.BlockSpec(target.shape, lambda i, *_: (0, 0)))
    args = list(blocks) + [target]
    if start is not None:
        specs.append(pl.BlockSpec((batch * LANES, columns), lambda i, *_: (i, 0)))
        args.append(start)
    if final:
        out_spec = pl.BlockSpec((fields, low * batch, 2, columns), lambda i, *_: (0, i, 0, 0))
        out_shape = jax.ShapeDtypeStruct((fields, low * count, 2, columns), jnp.bfloat16)
    else:
        out_spec = pl.BlockSpec((batch * LANES, columns), lambda i, *_: (i, 0))
        out_shape = jax.ShapeDtypeStruct((LANES * count, columns), jnp.bfloat16)
    rows = target.shape[0]
    return pl.pallas_call(
        functools.partial(
            place_kernel,
            pieces=len(blocks),
            final=final,
            with_start=start is not None,
            split=split,
            depths=depths,
            low=low,
            batch=batch,
        ),
        grid_spec=pltpu.PrefetchScalarGridSpec(
            num_scalar_prefetch=1,
            grid=(count // batch,),
            in_specs=specs,
            out_specs=out_spec,
            scratch_shapes=[
                pltpu.VMEM((rows, columns // split), jnp.bfloat16),
                pltpu.VMEM((low, rows, LANES), jnp.float32),
                pltpu.VMEM((batch * LANES, rows), jnp.bfloat16),
            ],
        ),
        out_shape=out_shape,
        name="place",
    )(rank, *args)


def chunk_tiles(tiles):
    first = max(1, tiles * 2 // 5)
    return [first, tiles - first] if tiles > first else [first]


def partner(me, piece, groups, levels, back):
    fast = 2 * levels if groups % 2 == 0 else levels
    slow = groups * levels // fast
    far = piece // fast
    high = (me // fast + (slow - far if back else far)) % slow
    near = me % fast
    if fast & (fast - 1) == 0:
        low = near ^ (piece % fast)
    else:
        low = (near + (fast - piece % fast if back else piece % fast)) % fast
    return high * fast + low


def late_pieces(groups, levels):
    fast = 2 * levels if groups % 2 == 0 else levels
    half = groups * levels // fast // 2
    return [p for p in range(1, groups * levels) if p // fast == half]


def shift(pieces, groups, levels):
    owners = groups * levels
    moved = [pieces[0]]
    for piece in range(1, owners):
        pairs = [(i, partner(i, piece, groups, levels, False)) for i in range(owners)]
        moved.append(lax.ppermute(pieces[piece], AXES, pairs))
    return moved


def ordered(keys):
    rank = jnp.sum((keys[:, None, :] < keys[:, :, None]).astype(jnp.int32), 2)
    spot = jnp.arange(keys.shape[1], dtype=jnp.int32)
    chosen = jnp.where(rank[:, :, None] == spot, keys[:, :, None], 0)
    return jnp.sum(chosen, 1), rank


def profiles(tiles, count):
    shares = [(0.4, 1.0), (0.6, 0.95), (0.8, 0.8), (1.0, 0.6)]
    small = []
    for tile in range(tiles):
        share = next(share for bound, share in shares if tile + 0.5 < bound * tiles)
        small.append(min(count, math.ceil(share * count - 1e-6)))
    return [small, [count] * tiles]


def local(grid, lat_order, wave_order, trim, legendre, modes_in, modes_out, implicit):
    fields, lats, _, lon_count = grid.shape
    per_device, row_count, lat_count = legendre.shape
    levels = lax.axis_size("lev")
    groups = lax.axis_size("wave")
    owners = groups * levels
    low = LANES // (2 * fields)
    count = lats // low
    share = per_device // levels
    tiles = -(-share // TILE)
    group = lax.axis_index("wave")
    me = group * levels + lax.axis_index("lev")

    def tables():
        trims = trim[wave_order].reshape(groups, per_device)
        near = jnp.arange(per_device, dtype=jnp.int32)
        keys = (trims * per_device + near) * row_count + wave_order.reshape(groups, per_device)
        keys, _ = ordered(keys)
        keys = keys.reshape(groups, share, levels).transpose(0, 2, 1).reshape(owners, share)
        slot = jnp.arange(tiles * TILE, dtype=jnp.int32)
        keys = keys[:, jnp.minimum(slot, share - 1)]
        owner_near = keys // row_count % per_device
        table = (lat_count - 1 - lat_order).reshape(groups, lats)
        table, rank = ordered(table * lats + jnp.arange(lats, dtype=jnp.int32))
        slot_lats = lat_count - 1 - table // lats
        rank = lax.dynamic_slice_in_dim(rank, group, 1)[0]

        mine = lax.dynamic_slice_in_dim(keys, me, 1)[0]
        meta = jnp.stack(
            [mine % row_count, mine // (row_count * per_device), mine // row_count % per_device]
        )
        first_column = (jnp.arange(owners, dtype=jnp.int32) // levels * (2 * per_device))[:, None]
        columns = jnp.where(slot < share, first_column + 2 * owner_near, -4 * per_device * owners)

        piece = jnp.arange(owners, dtype=jnp.int32)
        natural = jnp.stack([piece, piece])
        paired = jnp.stack(
            [partner(me, piece, groups, levels, back) for back in (True, False)]
        )
        peers = [natural, paired]

        metas, targets, first = [], [], 0
        for which, size in enumerate(sizes):
            span = slice(first * TILE, (first + size) * TILE)
            shape = (owners, size, 2, TILE)
            goal = columns if which == 0 else columns[paired[0]]
            goal = goal[:, span].reshape(owners, size, 1, TILE)
            goal = goal + jnp.arange(2, dtype=jnp.int32)[:, None]
            targets.append(jnp.broadcast_to(goal, shape).reshape(-1, 1))
            metas.append(meta[:, span])
            first += size

        slots = slot_lats.reshape(groups * count, low).T
        select = (slots[:, :, None] == jnp.arange(lat_count, dtype=jnp.int32)).astype(jnp.bfloat16)
        same = jnp.eye(2, dtype=jnp.bfloat16)
        split_in = modes_in.reshape(-1, levels, fields)
        into = jnp.einsum("klf,cd->ckldf", split_in, same)
        into = jnp.repeat(into.reshape(2 * levels * fields, 2 * levels * fields), 2, axis=1)
        split_out = modes_out.reshape(levels, fields, -1)
        back = jnp.einsum("lfk,cd->lcfdk", split_out, same)
        back = jnp.repeat(back.reshape(2 * levels * fields, 2 * levels * fields), 2, axis=0)
        tall = jnp.concatenate([implicit, implicit])[:, None]
        turned = jnp.swapaxes(legendre, 1, 2)
        return metas, peers, rank, targets, (turned, select, into, back, tall)

    def exchange(blocks):
        if len(blocks) == 1:
            return [lax.all_to_all(blocks[0], AXES, split_axis=0, concat_axis=0, tiled=True)]
        return shift(blocks, groups, levels)

    def run(depths):
        depths = [tuple(depths[span]) for span in spans]
        sent = []
        for which, freq in enumerate(freqs):
            sent.append(dft(grid, notes, freq, depths[which], owners, lats, low, which > 0))
        metas, peers, rank, targets, weights = tables()
        received = []
        for blocks in sent:
            received.append(exchange(blocks))
        returned = []
        for which, blocks in enumerate(received):
            made = middle(
                blocks, metas[which], peers[which], *weights, levels, depths[which], count
            )
            returned.append(exchange(made))
        result = None
        for which, blocks in enumerate(returned):
            last = which == len(returned) - 1
            late = late_pieces(groups, levels) if len(blocks) > 1 else []
            parts = [[p for p in range(len(blocks)) if p not in late], late]
            parts = [part for part in parts if part]
            rows = targets[which].reshape(len(blocks), -1)
            for part in parts:
                target = jnp.concatenate([rows[p] for p in part]).reshape(-1, 1)
                if len(part) == len(blocks):
                    target = targets[which]
                result = place(
                    [blocks[p] for p in part], rank, target, result, lon_count, fields, low,
                    last and part is parts[-1], depths[which],
                )
        return result

    sizes = chunk_tiles(tiles)
    spans, first = [], 0
    for size in sizes:
        spans.append(slice(first, first + size))
        first += size
    small, full = profiles(tiles, count)
    *freqs, notes = plan(
        wave_order, trim, lat_order, groups, levels, share, low, small, sizes
    )
    if PROFILE is not None:
        return run((small, full)[PROFILE])
    return lax.cond(notes[1, 0] > 0, lambda: run(small), lambda: run(full))


PROFILE = None


def solution(mesh):
    in_specs = (
        P(("member", "lev"), "wave", None, None),
        P(),
        P(),
        P(),
        P("wave", None, None),
        P(),
        P(),
        P(),
    )
    out_specs = P(("member", "lev"), "wave", None, None)
    return jax.shard_map(local, mesh=mesh, in_specs=in_specs, out_specs=out_specs, check_vma=False)
```

```python
import functools
import math

import jax
import jax.numpy as jnp
from jax import lax
from jax.experimental import pallas as pl
from jax.experimental.pallas import tpu as pltpu
from jax.sharding import PartitionSpec as P


LBLK = 64
LANES = 128
TILE = 8
AXES = ("wave", "lev")
NT = (((1,), (1,)), ((), ()))
NN = (((1,), (0,)), ((), ()))


def dot(a, b, dims=NN):
    return lax.dot_general(a, b, dims, preferred_element_type=jnp.float32)


def cosine_rows(freq_ref, first, count, lon_count):
    freq = freq_ref[pl.ds(first, count), :]
    row = lax.broadcasted_iota(jnp.int32, (count, 1), 0) + first
    phase = ((row // TILE) % 2).astype(jnp.float32) * (lon_count // 4)
    longitude = lax.broadcasted_iota(jnp.int32, (1, lon_count), 1).astype(jnp.float32)
    turns = freq * longitude + phase
    whole = jnp.floor(turns * (1.0 / lon_count) + 0.5)
    angle = 0.5 * math.pi - jnp.abs(turns - whole * lon_count) * (2.0 * math.pi / lon_count)
    square = angle * angle
    scale = 1.0 / math.sqrt(lon_count)
    value = square * (scale / 362880.0) - scale / 5040.0
    for term in (1.0 / 120.0, -1.0 / 6.0, 1.0):
        value = value * square + term * scale
    return (value * angle).astype(jnp.bfloat16)


def units(depths):
    starts, first = [], 0
    for depth in depths:
        starts.append((first, first + depth))
        first += 2 * depth
    return starts, first


def dft_kernel(lats_ref, *refs, depths, pairs, slots):
    views, freq, outs, table = refs[:slots], refs[slots], refs[slots + 1 : -1], refs[-1]
    fields, lon_count = views[0].shape[0], views[0].shape[3]
    step = pl.program_id(0)
    starts, _ = units(depths)

    @pl.when(step == 0)
    def _():
        rows = 4 * TILE if table.shape[0] % (4 * TILE) == 0 else 2 * TILE

        @pl.loop(0, table.shape[0] // rows)
        def _(i):
            first = pl.multiple_of(i * rows, rows)
            table[pl.ds(first, rows), :] = cosine_rows(freq, first, rows, lon_count)

    values = [view[:, 0].reshape(2 * fields, lon_count) for view in views]
    spectra = dot(table[...], jnp.concatenate(values, 0), NT)
    spectra = spectra.reshape(-1, len(depths), 2, TILE, pairs * LANES)

    def store(tile, pair, where):
        for part in range(2):
            block = spectra[:, tile, part, :, pair * LANES : (pair + 1) * LANES]
            block = block.astype(jnp.bfloat16)
            for piece, out in enumerate(outs):
                out[0, starts[tile][part] + where] = block[piece]

    for pair in range(pairs):
        where = step * pairs + pair
        for tile, depth in enumerate(depths):
            pl.when(where < depth)(functools.partial(store, tile, pair, where))


def dft(grid, order, freq, depths, owners, lats, low):
    fields, _, _, lon_count = grid.shape
    count = lats // low
    pairs = 2 if count % 2 == 0 else 1
    slots = pairs * low
    shape = (1, units(depths)[1], TILE, LANES)

    def view(slot):
        return pl.BlockSpec(
            (fields, 1, 2, lon_count),
            lambda i, order: (0, order[0, i * slots + slot], 0, 0),
        )

    return pl.pallas_call(
        functools.partial(dft_kernel, depths=depths, pairs=pairs, slots=slots),
        grid_spec=pltpu.PrefetchScalarGridSpec(
            num_scalar_prefetch=1,
            grid=(count // pairs,),
            in_specs=[view(slot) for slot in range(slots)]
            + [pl.BlockSpec(freq.shape, lambda i, _: (0, 0))],
            out_specs=[pl.BlockSpec(shape, lambda i, _: (0, 0, 0, 0))] * owners,
            scratch_shapes=[pltpu.VMEM((freq.shape[0], lon_count), jnp.bfloat16)],
        ),
        out_shape=[jax.ShapeDtypeStruct(shape, jnp.bfloat16)] * owners,
        name="dft",
    )(order, *([grid] * slots), freq)


def as_column(row):
    return jnp.broadcast_to(row, (LANES, row.shape[1])).T[:, :1]


def plan_kernel(
    waves_ref, trim_ref, lats_ref, *outs, groups, levels, share, low, small, sizes, axes
):
    freqs, notes = outs[:-1], outs[-1]
    total = waves_ref.shape[0]
    near_count = total // groups
    waves = waves_ref[...].reshape(1, -1).astype(jnp.float32)
    lane = lax.broadcasted_iota(jnp.int32, (1, total), 1).astype(jnp.float32)
    number = lax.broadcasted_iota(jnp.int32, (total, 1), 0).astype(jnp.float32)
    trim_column = as_column(trim_ref[...].reshape(1, -1).astype(jnp.float32))
    trims = jnp.sum(jnp.where(number == waves, trim_column, 0.0), 0, keepdims=True)
    base = jnp.floor((lane + 0.5) * (1.0 / near_count)) * near_count
    keys = (base * 8.0 + trims * near_count) + (lane - base)
    rank = jnp.sum(jnp.where(as_column(keys) < keys, 1.0, 0.0), 0, keepdims=True)

    group = lax.axis_index(axes[0])
    me = group * levels + lax.axis_index(axes[1])
    first = 0
    for freq, size in zip(freqs, sizes):
        rows = size * 2 * TILE
        row = lax.broadcasted_iota(jnp.int32, (rows, 1), 0)
        tile, wave = row // (2 * TILE), row % TILE
        slot = jnp.minimum((first + tile) * TILE + wave, share - 1) * levels
        slot = slot.astype(jnp.float32)
        for piece in range(groups * levels):
            owner = partner(me, jnp.int32(piece), groups, levels, False)
            start = ((owner // levels) * near_count + owner % levels).astype(jnp.float32)
            chosen = jnp.where(rank == slot + start, waves, 0.0)
            freq[piece * rows : (piece + 1) * rows, :] = jnp.sum(chosen, 1, keepdims=True)
        first += size

    lats = lats_ref[...].reshape(1, -1).astype(jnp.float32)
    lat_count = lats.shape[1]
    slots = lat_count // groups
    lane = lax.broadcasted_iota(jnp.int32, (1, lat_count), 1).astype(jnp.float32)
    origin = jnp.floor((lane + 0.5) * (1.0 / slots)) * slots
    owner = lax.broadcasted_iota(jnp.int32, (groups, 1), 0).astype(jnp.float32) * slots == origin
    fits = jnp.full((1, 1), 1, jnp.int32)
    for tile, depth in enumerate(small):
        spot = (rank - base) == float(min(tile * TILE, share - 1) * levels)
        least = jnp.min(jnp.where(spot, trims, 8.0), 1, keepdims=True)
        needed = jnp.where(owner & (lats >= LBLK * least), 1.0, 0.0)
        needed = jnp.max(jnp.sum(needed, 1, keepdims=True), 0, keepdims=True)
        fits = fits * jnp.where(needed <= float(low * depth), 1, 0)

    keys = (origin + slots) * lat_count - lats
    place_of = jnp.sum(jnp.where(as_column(keys) < keys, 1.0, 0.0), 0, keepdims=True)
    spot = lax.broadcasted_iota(jnp.int32, (1, LANES), 1).astype(jnp.float32)
    start = (group * slots).astype(jnp.float32)
    index = lax.broadcasted_iota(jnp.int32, (lat_count, 1), 0).astype(jnp.float32) - start
    chosen = jnp.where(as_column(place_of) - start == spot, index, 0.0)
    order = jnp.sum(chosen, 0, keepdims=True)
    notes[0:1, :] = order.astype(jnp.int32)
    notes[1:2, :] = jnp.broadcast_to(fits, (1, LANES))


def plan(wave_order, trim, lat_order, groups, levels, share, low, small, sizes):
    owners = groups * levels
    return pl.pallas_call(
        functools.partial(
            plan_kernel, groups=groups, levels=levels, share=share, low=low, small=small,
            sizes=sizes, axes=AXES,
        ),
        out_shape=[
            jax.ShapeDtypeStruct((owners * size * 2 * TILE, 1), jnp.float32) for size in sizes
        ]
        + [jax.ShapeDtypeStruct((TILE, LANES), jnp.int32)],
        name="plan",
    )(wave_order, trim, lat_order)


def middle_kernel(meta, peers, *refs, levels, owners, depths, count):
    data, refs = refs[:owners], refs[owners:]
    legendre, select, into, back, implicit = refs[:5]
    out, (held, made) = refs[5:-2], refs[-2:]
    each = owners // len(out)
    step = pl.program_id(0)
    starts, _ = units(depths)
    groups = owners // levels
    half = LANES // 2
    lat_count, row_count = legendre.shape[1], legendre.shape[2]

    slots = groups * count
    tile_rows = 2 * levels * slots * TILE

    def place_of(owner, tile, part, first, rows):
        near = ((owner % levels) * 2 + part) * groups + owner // levels
        start = near * (count * TILE) + (tile * tile_rows + first * TILE)
        return pl.ds(pl.multiple_of(start, TILE), rows * TILE)

    @pl.when(step == 0)
    def _():
        for piece in range(owners):
            owner = peers[0, piece]
            for tile, depth in enumerate(depths):
                for part in range(2):
                    first = starts[tile][part]
                    block = data[piece][0, first : first + depth]
                    block = block.astype(jnp.float32).reshape(-1, LANES)
                    held[place_of(owner, tile, part, 0, depth), :] = block
                    if depth < count:
                        rest = count - depth
                        empty = jnp.zeros((rest * TILE, LANES), jnp.float32)
                        held[place_of(owner, tile, part, depth, rest), :] = empty

    origin = (step // TILE) * tile_rows + step % TILE

    def column(combo):
        return pl.ds(origin + combo * slots * TILE, slots, stride=TILE)

    wavenum, trim = meta[0, step], meta[1, step]
    north, south = [], []
    for combo in range(2 * levels):
        block = held[column(combo), :]
        turned = block.T
        north.append(turned[:half])
        south.append(turned[half:])
    first = jnp.concatenate(north, 0).astype(jnp.bfloat16)
    second = jnp.concatenate(south, 0).astype(jnp.bfloat16)
    basis = legendre[0]
    ordered = dot(first, select[0]) + dot(second, select[1])
    latitude = lax.broadcasted_iota(jnp.int32, (1, lat_count), 1)
    keep = latitude >= LBLK * trim
    ordered = jnp.where(keep, ordered, 0.0).astype(jnp.bfloat16)
    coeffs = dot(ordered, basis)
    row = lax.broadcasted_iota(jnp.int32, (1, row_count), 1)
    degree = (row + wavenum).astype(jnp.float32)
    factor = degree * (degree + 1.0) * (1.0 / float(row_count * (row_count - 1)))
    south_side = lax.broadcasted_iota(jnp.int32, (coeffs.shape[0], 1), 0) % 2
    flip = (south_side * (row % 2)) == 1
    coeffs = jnp.where(flip, -coeffs, coeffs).astype(jnp.bfloat16)
    modal = dot(into[...], coeffs)
    scaled = (modal / (1.0 + factor * implicit[...])).astype(jnp.bfloat16)
    solved = dot(back[...], scaled)
    solved = jnp.where(row + wavenum < row_count, solved, 0.0)
    solved = jnp.where(flip, -solved, solved).astype(jnp.bfloat16)
    sides = dot(solved, basis, NT)
    sides = jnp.where(keep, sides, 0.0).astype(jnp.bfloat16)
    first = dot(sides, select[0], NT)
    second = dot(sides, select[1], NT)
    for combo in range(2 * levels):
        span = slice(combo * half, (combo + 1) * half)
        block = jnp.concatenate([first[span], second[span]], 0).T
        made[column(combo), :] = block

    @pl.when(step == pl.num_programs(0) - 1)
    def _():
        for piece in range(owners):
            owner = peers[1, piece]
            for tile, depth in enumerate(depths):
                for part in range(2):
                    first = starts[tile][part]
                    block = made[place_of(owner, tile, part, 0, depth), :]
                    block = block.reshape(depth, TILE, LANES).astype(jnp.bfloat16)
                    out[piece // each][piece % each, first : first + depth] = block


def middle(
    data, meta, peers, legendre, select, into, back, implicit, levels, depths, count, joint
):
    owners = len(data)
    made = [data[0]] * owners
    if joint:
        made = [jax.ShapeDtypeStruct((owners,) + data[0].shape[1:], jnp.bfloat16)]
    whole = lambda a: pl.BlockSpec(a.shape, lambda i, *_: (0,) * a.ndim)
    rows = owners * 2 * count * TILE * len(depths)
    return pl.pallas_call(
        functools.partial(
            middle_kernel, levels=levels, owners=owners, depths=depths, count=count
        ),
        grid_spec=pltpu.PrefetchScalarGridSpec(
            num_scalar_prefetch=2,
            grid=(len(depths) * TILE,),
            in_specs=[whole(a) for a in data]
            + [pl.BlockSpec((1,) + legendre.shape[1:], lambda i, meta, _: (meta[2, i], 0, 0))]
            + [whole(a) for a in (select, into, back, implicit)],
            out_specs=[whole(a) for a in made],
            scratch_shapes=[pltpu.VMEM((rows, LANES), jnp.float32)] * 2,
        ),
        out_shape=[jax.ShapeDtypeStruct(a.shape, jnp.bfloat16) for a in made],
        name="middle",
    )(meta, peers, *data, legendre, select, into, back, implicit)


def place_kernel(rank, *refs, pieces, final, with_start, split, depths, low, batch):
    blocks, refs = refs[:pieces], refs[pieces:]
    target, refs = refs[0], refs[1:]
    start = refs[0] if with_start else None
    out, table, gathered, held = refs[-4:]
    per = table.shape[0] // split
    each = blocks[0].shape[0]
    span_rows = 2 * TILE * len(depths)
    span = LANES // low
    starts, _ = units(depths)
    step = pl.program_id(0)

    @pl.when(step == 0)
    def _():
        column = lax.broadcasted_iota(jnp.int32, table.shape, 1)
        goal = target[...]
        for piece in range(split):
            rows = slice(piece * per, (piece + 1) * per)
            wanted = goal[rows] - piece * table.shape[1]
            table[rows, :] = jnp.where(column[rows] == wanted, 1.0, 0.0).astype(jnp.bfloat16)

    lane = lax.broadcasted_iota(jnp.int32, (1, LANES), 1) // span

    def turn(item):
        merged = None
        for slot in range(low):
            index = rank[(step * batch + item) * low + slot]
            where, side = index // low, index % low
            for piece in range(each * pieces):
                for tile, depth in enumerate(depths):
                    near = jnp.minimum(where, depth - 1)
                    for part in range(2):
                        unit = starts[tile][part] + near
                        block = blocks[piece // each][piece % each, unit].astype(jnp.float32)
                        if depth < rank.shape[0] // low:
                            block = jnp.where(where < depth, block, 0.0)
                        first = piece * span_rows + (2 * tile + part) * TILE
                        gathered[slot, first : first + TILE, :] = block
            values = pltpu.roll(gathered[slot], ((slot - side) % low) * span, 1)
            merged = values if merged is None else jnp.where(lane == slot, values, merged)
        return merged.T.astype(jnp.bfloat16)

    if final:
        rows = jnp.concatenate([turn(item) for item in range(batch)], 0)
    else:

        @pl.loop(0, batch)
        def _(item):
            held[pl.ds(pl.multiple_of(item * LANES, LANES), LANES), :] = turn(item)

        rows = held[...]
    placed = []
    for piece in range(split):
        part = slice(piece * per, (piece + 1) * per)
        placed.append(dot(rows[:, part], table[part, :]))
    placed = jnp.concatenate(placed, 1) if split > 1 else placed[0]
    placed = placed.astype(jnp.bfloat16)
    if with_start:
        placed = placed + start[...]
    if not final:
        out[...] = placed
        return
    fields = out.shape[0]
    for slot in range(batch * low):
        block = placed[slot * 2 * fields : (slot + 1) * 2 * fields]
        out[:, slot] = block.reshape(fields, 2, block.shape[1])


def place(blocks, rank, target, start, columns, fields, low, final, depths):
    each = blocks[0].shape[0]
    owners = each * len(blocks)
    count = rank.shape[0] // low
    batch = max(b for b in (1, 2, 4) if count % b == 0)
    split = 2 if len(blocks) == 1 and owners % 2 == 0 and (columns // 2) % LANES == 0 else 1
    specs = [pl.BlockSpec(b.shape, lambda i, *_: (0, 0, 0, 0)) for b in blocks]
    specs.append(pl.BlockSpec(target.shape, lambda i, *_: (0, 0)))
    args = list(blocks) + [target]
    if start is not None:
        specs.append(pl.BlockSpec((batch * LANES, columns), lambda i, *_: (i, 0)))
        args.append(start)
    if final:
        out_spec = pl.BlockSpec((fields, low * batch, 2, columns), lambda i, *_: (0, i, 0, 0))
        out_shape = jax.ShapeDtypeStruct((fields, low * count, 2, columns), jnp.bfloat16)
    else:
        out_spec = pl.BlockSpec((batch * LANES, columns), lambda i, *_: (i, 0))
        out_shape = jax.ShapeDtypeStruct((LANES * count, columns), jnp.bfloat16)
    rows = target.shape[0]
    return pl.pallas_call(
        functools.partial(
            place_kernel,
            pieces=len(blocks),
            final=final,
            with_start=start is not None,
            split=split,
            depths=depths,
            low=low,
            batch=batch,
        ),
        grid_spec=pltpu.PrefetchScalarGridSpec(
            num_scalar_prefetch=1,
            grid=(count // batch,),
            in_specs=specs,
            out_specs=out_spec,
            scratch_shapes=[
                pltpu.VMEM((rows, columns // split), jnp.bfloat16),
                pltpu.VMEM((low, rows, LANES), jnp.float32),
                pltpu.VMEM((batch * LANES, rows), jnp.bfloat16),
            ],
        ),
        out_shape=out_shape,
        name="place",
    )(rank, *args)


def chunk_tiles(tiles):
    first = max(1, tiles * 2 // 5)
    return [first, tiles - first] if tiles > first else [first]


def partner(me, piece, groups, levels, back):
    fast = 2 * levels if groups % 2 == 0 else levels
    slow = groups * levels // fast
    far = piece // fast
    high = (me // fast + (slow - far if back else far)) % slow
    near = me % fast
    if fast & (fast - 1) == 0:
        low = near ^ (piece % fast)
    else:
        low = (near + (fast - piece % fast if back else piece % fast)) % fast
    return high * fast + low


def late_pieces(groups, levels):
    fast = 2 * levels if groups % 2 == 0 else levels
    half = groups * levels // fast // 2
    return [p for p in range(1, groups * levels) if p // fast >= half]


def shift(pieces, groups, levels):
    owners = groups * levels
    moved = [pieces[0]]
    for piece in range(1, owners):
        pairs = [(i, partner(i, piece, groups, levels, False)) for i in range(owners)]
        moved.append(lax.ppermute(pieces[piece], AXES, pairs))
    return moved


def ordered(keys):
    rank = jnp.sum((keys[:, None, :] < keys[:, :, None]).astype(jnp.int32), 2)
    spot = jnp.arange(keys.shape[1], dtype=jnp.int32)
    chosen = jnp.where(rank[:, :, None] == spot, keys[:, :, None], 0)
    return jnp.sum(chosen, 1), rank


def profiles(tiles, count):
    shares = [(0.4, 1.0), (0.6, 0.95), (0.8, 0.8), (1.0, 0.6)]
    small = []
    for tile in range(tiles):
        share = next(share for bound, share in shares if tile + 0.5 < bound * tiles)
        small.append(min(count, math.ceil(share * count - 1e-6)))
    return [small, [count] * tiles]


def local(grid, lat_order, wave_order, trim, legendre, modes_in, modes_out, implicit):
    fields, lats, _, lon_count = grid.shape
    per_device, row_count, lat_count = legendre.shape
    levels = lax.axis_size("lev")
    groups = lax.axis_size("wave")
    owners = groups * levels
    low = LANES // (2 * fields)
    count = lats // low
    share = per_device // levels
    tiles = -(-share // TILE)
    group = lax.axis_index("wave")
    me = group * levels + lax.axis_index("lev")

    def tables():
        trims = trim[wave_order].reshape(groups, per_device)
        near = jnp.arange(per_device, dtype=jnp.int32)
        keys = (trims * per_device + near) * row_count + wave_order.reshape(groups, per_device)
        keys, _ = ordered(keys)
        keys = keys.reshape(groups, share, levels).transpose(0, 2, 1).reshape(owners, share)
        slot = jnp.arange(tiles * TILE, dtype=jnp.int32)
        keys = keys[:, jnp.minimum(slot, share - 1)]
        owner_near = keys // row_count % per_device
        table = (lat_count - 1 - lat_order).reshape(groups, lats)
        table, rank = ordered(table * lats + jnp.arange(lats, dtype=jnp.int32))
        slot_lats = lat_count - 1 - table // lats
        rank = lax.dynamic_slice_in_dim(rank, group, 1)[0]

        mine = lax.dynamic_slice_in_dim(keys, me, 1)[0]
        meta = jnp.stack(
            [mine % row_count, mine // (row_count * per_device), mine // row_count % per_device]
        )
        first_column = (jnp.arange(owners, dtype=jnp.int32) // levels * (2 * per_device))[:, None]
        columns = jnp.where(slot < share, first_column + 2 * owner_near, -4 * per_device * owners)

        piece = jnp.arange(owners, dtype=jnp.int32)
        paired = [partner(me, piece, groups, levels, back) for back in (True, False)]
        peers = [jnp.stack([paired[0], piece]), jnp.stack(paired)]

        metas, targets, first = [], [], 0
        for which, size in enumerate(sizes):
            span = slice(first * TILE, (first + size) * TILE)
            shape = (owners, size, 2, TILE)
            goal = columns if which == 0 else columns[paired[0]]
            goal = goal[:, span].reshape(owners, size, 1, TILE)
            goal = goal + jnp.arange(2, dtype=jnp.int32)[:, None]
            targets.append(jnp.broadcast_to(goal, shape).reshape(-1, 1))
            metas.append(meta[:, span])
            first += size

        slots = slot_lats.reshape(groups * count, low).T
        select = (slots[:, :, None] == jnp.arange(lat_count, dtype=jnp.int32)).astype(jnp.bfloat16)
        same = jnp.eye(2, dtype=jnp.bfloat16)
        split_in = modes_in.reshape(-1, levels, fields)
        into = jnp.einsum("klf,cd->ckldf", split_in, same)
        into = jnp.repeat(into.reshape(2 * levels * fields, 2 * levels * fields), 2, axis=1)
        split_out = modes_out.reshape(levels, fields, -1)
        back = jnp.einsum("lfk,cd->lcfdk", split_out, same)
        back = jnp.repeat(back.reshape(2 * levels * fields, 2 * levels * fields), 2, axis=0)
        tall = jnp.concatenate([implicit, implicit])[:, None]
        turned = jnp.swapaxes(legendre, 1, 2)
        return metas, peers, rank, targets, (turned, select, into, back, tall)

    def exchange(blocks):
        if len(blocks) == 1:
            return [lax.all_to_all(blocks[0], AXES, split_axis=0, concat_axis=0, tiled=True)]
        return shift(blocks, groups, levels)

    def run(depths):
        depths = [tuple(depths[span]) for span in spans]
        sent = []
        for which, freq in enumerate(freqs):
            sent.append(dft(grid, notes, freq, depths[which], owners, lats, low))
        metas, peers, rank, targets, weights = tables()
        received = []
        for blocks in sent:
            received.append(shift(blocks, groups, levels))
        returned = []
        for which, blocks in enumerate(received):
            made = middle(
                blocks, metas[which], peers[which], *weights, levels, depths[which], count,
                which == 0,
            )
            returned.append(exchange(made))
        result = None
        for which, blocks in enumerate(returned):
            last = which == len(returned) - 1
            late = late_pieces(groups, levels) if len(blocks) > 1 else []
            parts = [[p for p in range(len(blocks)) if p not in late], late]
            parts = [part for part in parts if part]
            rows = targets[which].reshape(len(blocks), -1)
            for part in parts:
                target = jnp.concatenate([rows[p] for p in part]).reshape(-1, 1)
                if len(part) == len(blocks):
                    target = targets[which]
                result = place(
                    [blocks[p] for p in part], rank, target, result, lon_count, fields, low,
                    last and part is parts[-1], depths[which],
                )
        return result

    sizes = chunk_tiles(tiles)
    spans, first = [], 0
    for size in sizes:
        spans.append(slice(first, first + size))
        first += size
    small, full = profiles(tiles, count)
    *freqs, notes = plan(
        wave_order, trim, lat_order, groups, levels, share, low, small, sizes
    )
    if PROFILE is not None:
        return run((small, full)[PROFILE])
    return lax.cond(notes[1, 0] > 0, lambda: run(small), lambda: run(full))


PROFILE = None


def solution(mesh):
    in_specs = (
        P(("member", "lev"), "wave", None, None),
        P(),
        P(),
        P(),
        P("wave", None, None),
        P(),
        P(),
        P(),
    )
    out_specs = P(("member", "lev"), "wave", None, None)
    return jax.shard_map(local, mesh=mesh, in_specs=in_specs, out_specs=out_specs, check_vma=False)
```
